256 devices in a mesh: row: 16 (over z_hi, y, core), col: 16 (over x, z_lo).
Axes of the slice: x: 4, y: 4, z: 8 (z_hi: 2, z_lo: 4; z = z_hi * 4 + z_lo), core: 2. Of those that a mesh axis runs over, the one named last changes fastest.
Arguments:
- cost_rough: bfloat16 [33792, 33792], P('row', 'col'), may hold values from 0.0009994507 to 1
- land_mask: int32 [176, 192], P('row', 'col'), may hold values 0 or 1
- wage_start: float32 [176, 192, 256], P('row', 'col'), may hold values from -3 to 3
- tech_start: float32 [176, 192, 256], P('row', 'col'), may hold values from -3 to 3
- temp_start: float32 [176, 192, 256], P('row', 'col'), may hold values from -2.5 to 2.5
- damping: float32 [1], replicated, may hold values from 0.3 to 0.8
Outputs:
- wage_field: float32 [176, 192, 256], P('row', 'col')
- tech_field: float32 [176, 192, 256], P('row', 'col')
- temp_field: float32 [176, 192, 256], P('row', 'col')
The draws below stay inside these ranges and needn't reach their ends.
All inputs are finite; a program needn't handle non-finite values. No bound on the sum of `land_mask` on one device may be relied on, other than what follows from the above.
Results may differ from the reference program's by a relative error of at most 0.0003.
Values may be sent and summed in bfloat16 or wider, within the bound.
A program may use at most 128 MiB of HBM per device.

```python
import math
import jax
import jax.numpy as jnp
from jax import lax

LAT = 176
LON = 192
S = 256
ITERS = 3
CELLS = 33792
ELL = 44


def touch_ends(values, key, least, high):
    longest = values.shape.index(max(values.shape))
    spots = []
    for shift in (0, 1):
        where = [jax.random.randint(jax.random.fold_in(key, axis), (), 0, length) for axis, length in enumerate(values.shape)]
        where[longest] = (where[longest] + shift) % values.shape[longest]
        spots.append(tuple(where))
    return values.at[spots[0]].set(least).at[spots[1]].set(high)


def shard_levels(rng, dims, pieces, least, largest):
    def one(position, blocks):
        draws = jax.random.uniform(jax.random.fold_in(jax.random.fold_in(rng, 6), position), (blocks,), jnp.float32, least / len(pieces), largest / len(pieces))
        return jnp.repeat(jnp.exp(draws), dims[position] // blocks).reshape((-1,) + (1,) * (len(dims) - position - 1))

    gain = one(*pieces[0])
    for cut in pieces[1:]:
        gain = gain * one(*cut)
    return gain


def gaussian(stream_key, dims, deviation, limit, split=(), held_as=jnp.bfloat16):
    factor_of = shard_levels(stream_key, dims, split, -0.22, 0.18) if split else 1.0
    result = jax.random.normal(stream_key, dims, jnp.float32) * deviation * factor_of
    return jnp.minimum(jnp.maximum(result, -limit), limit).astype(held_as)


def setup_inputs(seed: int = 0) -> dict:
    keys = jax.random.split(jax.random.key(seed), 7)
    cost_rough = jnp.clip(jnp.exp(math.log(1.0) - 6.9083047 * jax.random.uniform(keys[0], (CELLS, CELLS), jnp.float32) ** shard_levels(keys[0], (CELLS, CELLS), ((0, 16), (1, 16)), -0.2, 0.2)), 0.0009994507, 1.0).astype(jnp.bfloat16)
    land_mask = touch_ends((jax.random.randint(keys[1], (LAT, LON), 0, 3) < 1).astype(jnp.int32), jax.random.fold_in(keys[1], 1), 0, 1)
    wage_start = gaussian(keys[2], (LAT, LON, S), 0.5, 3.0, ((0, 16), (1, 16)), jnp.float32)
    tech_start = gaussian(keys[3], (LAT, LON, S), 0.5, 3.0, ((0, 16), (1, 16)), jnp.float32)
    temp_start = gaussian(keys[4], (LAT, LON, S), 0.5, 2.5, ((0, 16), (1, 16)), jnp.float32)
    damping = jnp.clip(jax.random.uniform(keys[5], (1,), jnp.float32, 0.3, 0.8), 0.3, 0.8)
    return {"cost_rough": cost_rough, "land_mask": land_mask, "wage_start": wage_start, "tech_start": tech_start, "temp_start": temp_start, "damping": damping}


def cost_block(rough_block, destin, source):
    distance = (jnp.abs(destin[:, None] // LON - source[None, :] % LAT)
                + jnp.abs(destin[:, None] % LON - source[None, :] // LAT)).astype(jnp.float32)
    scaled = rough_block.astype(jnp.float32) * jnp.exp(-distance / ELL) / (ELL * ELL)
    return scaled.astype(jnp.bfloat16)


def laplace(field):
    padded = jnp.pad(field, ((1, 1), (1, 1), (0, 0)))
    return padded[2:, 1:-1] + padded[:-2, 1:-1] + padded[1:-1, 2:] + padded[1:-1, :-2] - 4.0 * field


def reference(cost_rough, land_mask, wage_start, tech_start, temp_start, damping):
    share = 0.25 + land_mask.astype(jnp.float32)[:, :, None]
    wage_field, tech_field, temp_field = wage_start, tech_start, temp_start
    blocks = cost_rough.reshape(LAT, LON, LAT * LON)
    source = jnp.arange(LAT * LON, dtype=jnp.int32)
    lat_rows = jnp.arange(LAT, dtype=jnp.int32)
    for iteration in range(ITERS):
        supply = (jnp.exp(tech_field - wage_field) * share).astype(jnp.bfloat16)
        columns = supply.transpose(1, 0, 2).reshape(LAT * LON, S)

        def block_access(pair):
            rough_block, lat_index = pair
            destin = lat_index * LON + jnp.arange(LON, dtype=jnp.int32)
            return jnp.dot(cost_block(rough_block, destin, source), columns, preferred_element_type=jnp.float32)

        access = lax.map(block_access, (blocks, lat_rows))
        target = 0.5 * (jnp.log(access) + tech_field)
        wage_field = wage_field + damping[0] * (target - wage_field)
        tech_next = tech_field + 0.2 * laplace(tech_field) - 0.05 * temp_field * temp_field
        temp_next = temp_field + 0.2 * laplace(temp_field) + 0.5 * share * jnp.tanh(wage_field)
        tech_field, temp_field = tech_next, temp_next
    return wage_field, tech_field, temp_field
```

```python
import jax
import jax.numpy as jnp
from jax import lax
from jax.experimental import pallas as pl
from jax.experimental.pallas import tpu as pltpu
from jax.sharding import PartitionSpec as P

LAT = 176
LON = 192
ITERS = 3
ELL = 44
A = 11
B = 12
S = 256
H = 128
BLOCK = 528
K = 2112
GROUP = 704
PIECE = 48
FLAT = 144
MESH = pl.DeviceIdType.MESH
f32 = jnp.float32
STEPS = 1024.0
MIDDLE = 8192.0
LN2 = 0.6931471805599453


def encode(value):
    code = jnp.log(jnp.maximum(value, 1e-30)) * (STEPS / LN2) + MIDDLE
    return jnp.round(jnp.clip(code, -32767.0, 32767.0)).astype(jnp.int32).astype(jnp.int16)


def decode(code):
    return jnp.exp((code.astype(jnp.int32).astype(f32) - MIDDLE) * (LN2 / STEPS))


def kernel(
    rough, share, wage0, tech0, temp0, damping,
    wage, tech, temp,
    stage, cost, near, pick, gathered, columns, piece, product, codes, landed, flat, zcodes, zlanded,
    access, padded, halo_out, halo_in, tech_new,
    stage_sem, ag_send, ag_recv, x_send, x_recv, z_send, z_recv, halo_send, halo_recv,
):
    row, col = lax.axis_index("row"), lax.axis_index("col")
    zh, y, core = row // 8, (row // 2) % 4, row % 2
    x, zl = col // 4, col % 4

    def at_row(zh_, y_, core_):
        return zh_ * 8 + (y_ % 4) * 2 + core_

    def at_col(x_, zl_):
        return (x_ % 4) * 4 + zl_ % 4

    partner = (at_row(zh, y, 1 - core), col)
    across = (at_row(1 - zh, y, core), col)
    y_up, y_down = (at_row(zh, y + 1, core), col), (at_row(zh, y + 3, core), col)
    x_up, x_down = (row, at_col(x + 1, zl)), (row, at_col(x + 3, zl))
    z_peers = [(row, at_col(x, zl + d)) for d in (1, 2, 3)]
    halo_peers = [((row + 1) % 16, col), ((row + 15) % 16, col), (row, (col + 1) % 16), (row, (col + 15) % 16)]
    peers = [partner, across, y_up, y_down, x_up, x_down] + z_peers + halo_peers

    def load_rough(a):
        return pltpu.make_async_copy(rough.at[pl.ds(a * LON, LON), :], stage.at[a], stage_sem.at[a])

    for a in range(A):
        load_rough(a).start()
    barrier = pltpu.get_barrier_semaphore()
    for peer in peers:
        pl.semaphore_signal(barrier, inc=1, device_id=peer, device_id_type=MESH)
    wage[...] = wage0[...]
    tech[...] = tech0[...]
    temp[...] = temp0[...]
    piece[...] = jnp.zeros_like(piece)
    flat[...] = jnp.zeros_like(flat)
    pl.semaphore_wait(barrier, len(peers))

    def slot(it, zh_, y_, core_):
        start = pl.multiple_of(at_row(zh_, y_, core_) * PIECE, 16)
        return gathered.at[it, :, :, pl.ds(start, PIECE), :]

    def half(it, h, zh_, y_, core_):
        start = pl.multiple_of(at_row(zh_, y_, core_) * PIECE, 16)
        return gathered.at[it, h, :, pl.ds(start, PIECE), :]

    def ag(it, k, ref, peer):
        return pltpu.make_async_remote_copy(
            src_ref=ref, dst_ref=ref, send_sem=ag_send.at[it, k], recv_sem=ag_recv.at[it, k],
            device_id=peer, device_id_type=MESH,
        )

    def own_copies(it):
        mine = slot(it, zh, y, core)
        return [ag(it, k, mine, peer) for k, peer in enumerate((partner, across, y_up, y_down))]

    def halo_copies(it):
        return [
            pltpu.make_async_remote_copy(
                src_ref=halo_out.at[it, d], dst_ref=halo_in.at[it, d],
                send_sem=halo_send.at[it, d], recv_sem=halo_recv.at[it, d],
                device_id=peer, device_id_type=MESH,
            )
            for d, peer in enumerate(halo_peers)
        ]

    def send_supply(it):
        for a in range(A):
            value = jnp.exp(tech[a] - wage[a]) * jnp.concatenate([share[a]] * 2, axis=1)
            for h in range(2):
                for g in range(3):
                    piece[h, g, 4 * a : 4 * a + 4, :] = value[4 * g : 4 * g + 4, h * H : h * H + H]
        start = pl.multiple_of(row * PIECE, 16)
        gathered[it, :, :, pl.ds(start, PIECE), :] = piece[...].astype(jnp.bfloat16)
        for copy in own_copies(it):
            copy.start()

    def send_halo(it):
        for f, field in enumerate((tech, temp)):
            halo_out[it, 0, f, 0:B, :] = field[A - 1]
            halo_out[it, 1, f, 0:B, :] = field[0]
            for a in range(A):
                halo_out[it, 2, f, a : a + 1, :] = field[a, B - 1 : B, :]
                halo_out[it, 3, f, a : a + 1, :] = field[a, 0:1, :]
        for copy in halo_copies(it):
            copy.start()

    halo_out[...] = jnp.zeros_like(halo_out)
    send_supply(0)
    send_halo(0)

    spot = lax.broadcasted_iota(jnp.int32, (1, 16 * PIECE), 1)
    device = jnp.zeros_like(spot)
    for r in range(1, 16):
        device = device + (spot >= PIECE * r).astype(jnp.int32)
    rest = spot - PIECE * device
    target = (rest & 3) * LAT + A * device + (rest >> 2)
    target = jnp.where(rest < 4 * A, target, -1)

    def pick_rows(i, _):
        start = pl.multiple_of(i * 16, 16)
        rows = i * 16 + lax.broadcasted_iota(jnp.int32, (16, 16 * PIECE), 0)
        pick[pl.ds(start, 16), :] = jnp.where(rows == target, 1.0, 0.0).astype(jnp.bfloat16)
        return 0

    lax.fori_loop(0, GROUP // 16, pick_rows, 0)

    column = lax.broadcasted_iota(jnp.int32, (1, K), 1)
    local_b = jnp.zeros_like(column)
    for b in range(1, B):
        local_b = local_b + (column >= LAT * b).astype(jnp.int32)
    source_a = column - LAT * local_b
    source_b = col * B + local_b

    def near_rows(i, _):
        start = pl.multiple_of(i * 16, 16)
        rows = i * 16 + lax.broadcasted_iota(jnp.int32, (16, K), 0)
        near[pl.ds(start, 16), :] = jnp.exp(jnp.abs(rows - source_b).astype(f32) * (-1.0 / ELL))
        return 0

    lax.fori_loop(0, LON // 16, near_rows, 0)

    def cost_latitude(a, _):
        load_rough(a).wait()
        lat = jnp.exp(jnp.abs(row * A + a - source_a).astype(f32) * (-1.0 / ELL)) * (1.0 / (ELL * ELL))

        def cost_rows(i, _):
            start = pl.multiple_of(i * 16, 16)
            put = pl.multiple_of(a * 48 + (i % 3) * 16, 16)
            value = stage[a, pl.ds(start, 16), :].astype(f32) * (lat * near[pl.ds(start, 16), :])
            cost[i // 3, pl.ds(put, 16), :] = value.astype(jnp.bfloat16)
            return 0

        return lax.fori_loop(0, LON // 16, cost_rows, 0)

    lax.fori_loop(0, A, cost_latitude, 0)

    def x_copy(it, k):
        return pltpu.make_async_remote_copy(
            src_ref=codes.at[k], dst_ref=landed.at[it, k],
            send_sem=x_send.at[it, k], recv_sem=x_recv.at[it, k],
            device_id=x_up if k % 2 == 0 else x_down, device_id_type=MESH,
        )

    def z_copy(it, d):
        return pltpu.make_async_remote_copy(
            src_ref=zcodes.at[(zl + d) % 4], dst_ref=zlanded.at[it, d - 1],
            send_sem=z_send.at[it, d - 1], recv_sem=z_recv.at[it, d - 1],
            device_id=z_peers[d - 1], device_id_type=MESH,
        )

    def iteration(it, _):
        pending = own_copies(it)

        def forward(k, ref, peer):
            copy = ag(it, k, ref, peer)
            copy.start()
            pending.append(copy)

        def arrived(k, ref, peer):
            ag(it, k, ref, peer).wait_recv()

        other = 1 - zh
        below, above, far = slot(it, zh, y + 3, core), slot(it, zh, y + 1, core), slot(it, zh, y + 2, core)
        arrived(2, below, y_down)
        forward(4, half(it, 0, zh, y + 3, core), y_up)
        forward(5, below, partner)
        arrived(3, above, y_up)
        forward(6, half(it, 1, zh, y + 1, core), y_down)
        forward(7, above, partner)
        theirs = slot(it, other, y, core)
        arrived(1, theirs, across)
        forward(8, theirs, y_up)
        forward(9, theirs, y_down)
        forward(10, theirs, partner)
        arrived(4, half(it, 0, zh, y + 2, core), y_down)
        arrived(6, half(it, 1, zh, y + 2, core), y_up)
        forward(11, far, partner)
        below, above, far = slot(it, other, y + 3, core), slot(it, other, y + 1, core), slot(it, other, y + 2, core)
        arrived(8, below, y_down)
        forward(12, half(it, 0, other, y + 3, core), y_up)
        forward(13, below, partner)
        arrived(9, above, y_up)
        forward(14, half(it, 1, other, y + 1, core), y_down)
        forward(15, above, partner)
        arrived(12, half(it, 0, other, y + 2, core), y_down)
        arrived(14, half(it, 1, other, y + 2, core), y_up)
        forward(16, far, partner)
        for k, zh_, dy in (
            (0, zh, 0), (5, zh, 3), (7, zh, 1), (10, other, 0), (11, zh, 2), (13, other, 3), (15, other, 1), (16, other, 2)
        ):
            arrived(k, slot(it, zh_, y + dy, 1 - core), partner)

        def select(g, _):
            start = pl.multiple_of(g * GROUP, 16)
            block = jnp.concatenate([gathered[it, 0, g], gathered[it, 1, g]], axis=1)
            columns[pl.ds(start, GROUP), :] = jnp.dot(pick[...], block, preferred_element_type=f32).astype(jnp.bfloat16)
            return 0

        lax.fori_loop(0, 3, select, 0)

        def multiply(n, x_):
            product[n] = jnp.dot(cost[x_ % 4], columns[...], preferred_element_type=f32)

        def rows_of(i):
            return pl.ds(pl.multiple_of(i * 48, 16), 48)

        def code_half(k, n, h):
            def some(i, _):
                codes[k, rows_of(i), :] = encode(product[n, rows_of(i), h * H : h * H + H])
                return 0

            lax.fori_loop(0, A, some, 0)
            x_copy(it, k).start()

        def code_sum(k, n, h, j):
            def some(i, _):
                value = product[n, rows_of(i), h * H : h * H + H] + decode(landed[it, j, rows_of(i), :])
                codes[k, rows_of(i), :] = encode(value)
                return 0

            lax.fori_loop(0, A, some, 0)
            x_copy(it, k).start()

        multiply(2, x + 2)
        code_half(0, 2, 0)
        code_half(1, 2, 1)
        multiply(1, x + 1)
        code_half(2, 1, 1)
        multiply(3, x + 3)
        code_half(3, 3, 0)
        x_copy(it, 0).wait_recv()
        code_sum(4, 1, 0, 0)
        x_copy(it, 1).wait_recv()
        code_sum(5, 3, 1, 1)
        multiply(0, x)

        for copy in halo_copies(it):
            copy.wait_recv()
        for f, field in enumerate((tech, temp)):
            low = jnp.where(row == 0, 0.0, halo_in[it, 0, f, 0:B, :])
            high = jnp.where(row == 15, 0.0, halo_in[it, 1, f, 0:B, :])
            for a in range(A):
                padded[f, a, 1 : 1 + B, :] = field[a]
                padded[f, a, 0:1, :] = jnp.where(col == 0, 0.0, halo_in[it, 2, f, a : a + 1, :])
                padded[f, a, B + 1 : B + 2, :] = jnp.where(col == 15, 0.0, halo_in[it, 3, f, a : a + 1, :])
            for a in range(A):
                centre = field[a]
                below_ = low if a == 0 else padded[f, a - 1, 1 : 1 + B, :]
                above_ = high if a == A - 1 else padded[f, a + 1, 1 : 1 + B, :]
                lap = above_ + below_ + padded[f, a, 2 : 2 + B, :] + padded[f, a, 0:B, :] - 4.0 * centre
                tech_new[f, a] = centre + 0.2 * lap
        for a in range(A):
            tech_new[0, a] = tech_new[0, a] - 0.05 * temp[a] * temp[a]

        for k in (2, 3, 4, 5):
            x_copy(it, k).wait_recv()
        for a in range(A):
            rows = slice(48 * a, 48 * a + 48)
            for h, j, k in ((0, 3, 4), (1, 2, 5)):
                value = product[0, rows, h * H : h * H + H] + decode(landed[it, j, rows, :]) + decode(landed[it, k, rows, :])
                for z in range(4):
                    flat[z, B * a : B * a + B, h * H : h * H + H] = value[B * z : B * z + B, :]
        for z in range(4):
            zcodes[z] = encode(flat[z])
        for d in (2, 1, 3):
            z_copy(it, d).start()
        for d in (1, 3, 2):
            z_copy(it, d).wait_recv()
        total = flat[zl]
        for d in (1, 2, 3):
            total = total + decode(zlanded[it, d - 1])
        access[...] = total

        for a in range(A):
            target_ = 0.5 * (jnp.log(access[B * a : B * a + B, :]) + tech[a])
            wage_a = wage[a] + damping[0] * (target_ - wage[a])
            wage[a] = wage_a
            both = jnp.concatenate([share[a]] * 2, axis=1)
            temp[a] = tech_new[1, a] + 0.5 * both * jnp.tanh(wage_a)
            tech[a] = tech_new[0, a]

        @pl.when(it < ITERS - 1)
        def _():
            send_supply(it + 1)
            send_halo(it + 1)

        for copy in pending:
            copy.wait_send()
        for k in range(6):
            x_copy(it, k).wait_send()
        for d in (1, 2, 3):
            z_copy(it, d).wait_send()
        for copy in halo_copies(it):
            copy.wait_send()
        return 0

    lax.fori_loop(0, ITERS, iteration, 0)


def local(cost_rough, land_mask, wage_start, tech_start, temp_start, damping):
    share = jnp.broadcast_to(0.25 + land_mask.astype(f32)[:, :, None], (A, B, H))
    field = jax.ShapeDtypeStruct((A, B, S), f32)
    vmem = pl.BlockSpec(memory_space=pltpu.VMEM)
    dma = pltpu.SemaphoreType.DMA
    return pl.pallas_call(
        kernel,
        out_shape=(field, field, field),
        in_specs=[pl.BlockSpec(memory_space=pl.ANY), vmem, vmem, vmem, vmem, pl.BlockSpec(memory_space=pltpu.SMEM)],
        out_specs=(vmem, vmem, vmem),
        scratch_shapes=[
            pltpu.VMEM((A, LON, K), jnp.bfloat16),
            pltpu.VMEM((4, BLOCK, K), jnp.bfloat16),
            pltpu.VMEM((LON, K), f32),
            pltpu.VMEM((GROUP, 16 * PIECE), jnp.bfloat16),
            pltpu.VMEM((ITERS, 2, 3, 16 * PIECE, H), jnp.bfloat16),
            pltpu.VMEM((K, S), jnp.bfloat16),
            pltpu.VMEM((2, 3, PIECE, H), f32),
            pltpu.VMEM((4, BLOCK, S), f32),
            pltpu.VMEM((6, BLOCK, H), jnp.int16),
            pltpu.VMEM((ITERS, 6, BLOCK, H), jnp.int16),
            pltpu.VMEM((4, FLAT, S), f32),
            pltpu.VMEM((4, FLAT, S), jnp.int16),
            pltpu.VMEM((ITERS, 3, FLAT, S), jnp.int16),
            pltpu.VMEM((FLAT, S), f32),
            pltpu.VMEM((2, A, 16, S), f32),
            pltpu.VMEM((ITERS, 4, 2, 16, S), f32),
            pltpu.VMEM((ITERS, 4, 2, 16, S), f32),
            pltpu.VMEM((2, A, B, S), f32),
            dma((A,)),
            dma((ITERS, 17)), dma((ITERS, 17)),
            dma((ITERS, 6)), dma((ITERS, 6)),
            dma((ITERS, 3)), dma((ITERS, 3)),
            dma((ITERS, 4)), dma((ITERS, 4)),
        ],
        compiler_params=pltpu.CompilerParams(collective_id=0, has_side_effects=True, vmem_limit_bytes=60 * 1024 * 1024),
    )(cost_rough, share, wage_start, tech_start, temp_start, damping)


def solution(mesh):
    in_specs = (
        P("row", "col"),
        P("row", "col"),
        P("row", "col", None),
        P("row", "col", None),
        P("row", "col", None),
        P(),
    )
    out_specs = (P("row", "col", None), P("row", "col", None), P("row", "col", None))
    return jax.shard_map(local, mesh=mesh, in_specs=in_specs, out_specs=out_specs, check_vma=False)
```

```python
import functools

import jax
import jax.numpy as jnp
from jax import lax
from jax.experimental import pallas as pl
from jax.experimental.pallas import tpu as pltpu
from jax.sharding import PartitionSpec as P

LAT = 176
LON = 192
ITERS = 3
ELL = 44
A = 11
B = 12
S = 256
H = 128
BLOCK = 528
K = 2112
PIECE = 48
SIDE = 8 * PIECE
WIDE = 3 * SIDE
WINDOWS = ((0, 768, 0), (640, 768, 64), (1408, 704, 0))
PARTS = ((0, 6), (6, 11))
FLAT = 144
MESH = pl.DeviceIdType.MESH
f32 = jnp.float32
STEPS = 1024.0
MIDDLE = 8192.0
LN2 = 0.6931471805599453


def encode(value):
    code = jnp.log(jnp.maximum(value, 1e-30)) * (STEPS / LN2) + MIDDLE
    return jnp.round(jnp.clip(code, -32767.0, 32767.0)).astype(jnp.int32).astype(jnp.int16)


def decode(code):
    return jnp.exp((code.astype(jnp.int32).astype(f32) - MIDDLE) * (LN2 / STEPS))


def kernel(
    rough, mask, wage0, tech0, temp0, damping,
    wage, tech, temp,
    stage, cost, near, pick, folded, share, gathered, piece, product, codes, landed, flat, zcodes, zlanded,
    padded, halo_out, halo_in, tech_new,
    start_sem, stage_sem, ag_send, ag_recv, x_send, x_recv, z_send, z_recv, halo_send, halo_recv,
):
    row, col = lax.axis_index("row"), lax.axis_index("col")
    zh, y, core = row // 8, (row // 2) % 4, row % 2
    x, zl = col // 4, col % 4

    def at_row(zh_, y_, core_):
        return zh_ * 8 + (y_ % 4) * 2 + core_

    def at_col(x_, zl_):
        return (x_ % 4) * 4 + zl_ % 4

    partner = (at_row(zh, y, 1 - core), col)
    across = (at_row(1 - zh, y, core), col)
    y_up, y_down = (at_row(zh, y + 1, core), col), (at_row(zh, y + 3, core), col)
    x_up, x_down = (row, at_col(x + 1, zl)), (row, at_col(x + 3, zl))
    z_peers = [(row, at_col(x, zl + d)) for d in (1, 2, 3)]
    halo_peers = [((row + 1) % 16, col), ((row + 15) % 16, col), (row, (col + 1) % 16), (row, (col + 15) % 16)]
    y_far = (at_row(zh, y + 2, core), col)
    peers = [partner, across, y_up, y_down, y_far, x_up, x_down] + z_peers + halo_peers

    def load_rough(a):
        return pltpu.make_async_copy(rough.at[pl.ds(a * LON, LON), :], stage.at[a], stage_sem.at[a])

    for a in range(A):
        load_rough(a).start()
    barrier = pltpu.get_barrier_semaphore()
    for peer in peers:
        pl.semaphore_signal(barrier, inc=1, device_id=peer, device_id_type=MESH)
    starts = [
        pltpu.make_async_copy(source, field, start_sem.at[n])
        for n, (source, field) in enumerate(((wage0, wage), (tech0, tech), (temp0, temp)))
    ]
    for copy in starts:
        copy.start()
    piece[...] = jnp.zeros_like(piece)
    flat[...] = jnp.zeros_like(flat)
    halo_out[...] = jnp.zeros_like(halo_out)
    diagonal = lax.broadcasted_iota(jnp.int32, (B, B), 0) == lax.broadcasted_iota(jnp.int32, (B, B), 1)
    for a in range(A):
        line = jnp.broadcast_to(mask[a : a + 1, :].astype(f32), (B, B))
        stand = jnp.sum(jnp.where(diagonal, line, 0.0), axis=1, keepdims=True)
        share[a] = jnp.broadcast_to(0.25 + stand, (B, S))

    spot = lax.broadcasted_iota(jnp.int32, (1, 16 * PIECE), 1)
    device = jnp.zeros_like(spot)
    for r in range(1, 16):
        device = device + (spot >= PIECE * r).astype(jnp.int32)
    rest = spot - PIECE * device
    target = (rest & 3) * LAT + A * device + (rest >> 2)
    target = jnp.where(rest < 4 * A, target, -4096)

    def pick_rows(i, _):
        start = pl.multiple_of(i * 16, 16)
        rows = i * 16 + lax.broadcasted_iota(jnp.int32, (16, 16 * PIECE), 0)
        for n, shift in enumerate((0, 64)):
            pick[n, pl.ds(start, 16), :] = jnp.where(rows == target + shift, 1.0, 0.0).astype(jnp.bfloat16)
        return 0

    lax.fori_loop(0, PIECE, pick_rows, 0)

    column = lax.broadcasted_iota(jnp.int32, (1, K), 1)
    local_b = jnp.zeros_like(column)
    for b in range(1, B):
        local_b = local_b + (column >= LAT * b).astype(jnp.int32)
    source_a = column - LAT * local_b
    source_b = col * B + local_b

    def near_rows(i, _):
        start = pl.multiple_of(i * 16, 16)
        rows = i * 16 + lax.broadcasted_iota(jnp.int32, (16, K), 0)
        near[pl.ds(start, 16), :] = jnp.exp(jnp.abs(rows - source_b).astype(f32) * (-1.0 / ELL))
        return 0

    lax.fori_loop(0, LON // 16, near_rows, 0)

    def cost_latitude(a, _):
        load_rough(a).wait()
        lat = jnp.exp(jnp.abs(row * A + a - source_a).astype(f32) * (-1.0 / ELL)) * (1.0 / (ELL * ELL))

        def cost_rows(i, _):
            start = pl.multiple_of(i * 16, 16)
            put = pl.multiple_of(a * 48 + (i % 3) * 16, 16)
            value = stage[a, pl.ds(start, 16), :].astype(f32) * (lat * near[pl.ds(start, 16), :])
            cost[i // 3, pl.ds(put, 16), :] = value.astype(jnp.bfloat16)
            return 0

        return lax.fori_loop(0, LON // 16, cost_rows, 0)

    lax.fori_loop(0, A, cost_latitude, 0)

    def fold(n):
        for g, (first, count, shift) in enumerate(WINDOWS):
            block = jnp.dot(
                cost[n, :, first : first + count], pick[1 if shift else 0, 0:count, :], preferred_element_type=f32
            ).astype(jnp.bfloat16)
            folded[n, 0, :, g * SIDE : g * SIDE + SIDE] = block[:, 0:SIDE]
            folded[n, 1, :, g * SIDE : g * SIDE + SIDE] = block[:, SIDE : 2 * SIDE]

    def slot(it, h, zh_, y_, core_):
        start = pl.multiple_of(((y_ % 4) * 2 + core_) * PIECE, 16)
        return gathered.at[it, zh_, h, :, pl.ds(start, PIECE), :]

    def ag(it, h, k, ref, peer):
        return pltpu.make_async_remote_copy(
            src_ref=ref, dst_ref=ref, send_sem=ag_send.at[it, h, k], recv_sem=ag_recv.at[it, h, k],
            device_id=peer, device_id_type=MESH,
        )

    other = 1 - zh

    def gather_copies(it, h):
        own, theirs = slot(it, h, zh, y, core), slot(it, h, other, y, core)
        table = [
            (0, own, across), (1, own, y_up), (2, own, y_down), (3, own, y_far), (4, own, partner),
            (5, theirs, y_up), (6, theirs, y_down), (7, theirs, y_far), (8, theirs, partner),
            (9, slot(it, h, zh, y + 3, core), partner), (10, slot(it, h, zh, y + 1, core), partner),
            (11, slot(it, h, zh, y + 2, core), partner),
            (12, slot(it, h, other, y + 3, core), partner), (13, slot(it, h, other, y + 1, core), partner),
            (14, slot(it, h, other, y + 2, core), partner),
        ]
        return [functools.partial(ag, it, h, *entry) for entry in table]

    def halo_copies(it):
        return [
            pltpu.make_async_remote_copy(
                src_ref=halo_out.at[it, d], dst_ref=halo_in.at[it, d],
                send_sem=halo_send.at[it, d], recv_sem=halo_recv.at[it, d],
                device_id=peer, device_id_type=MESH,
            )
            for d, peer in enumerate(halo_peers)
        ]

    def send_supply(it, h):
        for a in range(A):
            lanes = slice(h * H, h * H + H)
            value = jnp.exp(tech[a, :, lanes] - wage[a, :, lanes]) * share[a, :, lanes]
            for g in range(3):
                piece[h, g, 4 * a : 4 * a + 4, :] = value[4 * g : 4 * g + 4, :]
        start = pl.multiple_of((y * 2 + core) * PIECE, 16)
        gathered[it, zh, h, :, pl.ds(start, PIECE), :] = piece[h].astype(jnp.bfloat16)
        for copy in gather_copies(it, h)[0:5]:
            copy().start()

    def send_halo(it):
        for f, field in enumerate((tech, temp)):
            halo_out[it, 0, f, 0:B, :] = field[A - 1]
            halo_out[it, 1, f, 0:B, :] = field[0]
            for a in range(A):
                halo_out[it, 2, f, a : a + 1, :] = field[a, B - 1 : B, :]
                halo_out[it, 3, f, a : a + 1, :] = field[a, 0:1, :]
        for copy in halo_copies(it):
            copy.start()

    def supply_of(it, side):
        return jnp.concatenate([gathered[it, side, h].reshape(WIDE, H) for h in (0, 1)], axis=1)

    def gather(it, meanwhile):
        copies = [gather_copies(it, h) for h in (0, 1)]

        def arrived(h, k, zh_, dy, core_, peer):
            ag(it, h, k, slot(it, h, zh_, y + dy, core_), peer).wait_recv()

        def forward(h, *ks):
            for k in ks:
                copies[h][k]().start()

        def beside(h, side, first, then):
            arrived(h, first, side, 3, core, y_down)
            forward(h, then)
            arrived(h, first + 1, side, 1, core, y_up)
            forward(h, then + 1)

        def near_half(n, _):
            product[n] = jnp.dot(folded[(x + n) % 4, zh], supply_of(it, zh), preferred_element_type=f32)
            return 0

        def halves(first, last):
            lax.fori_loop(first, last, near_half, 0)

        for h in (0, 1):
            meanwhile(h, halves)
            beside(h, zh, 1, 9)
            arrived(h, 0, other, 0, core, across)
            forward(h, 5, 6, 7, 8)
            arrived(h, 3, zh, 2, core, y_far)
            forward(h, 11)
        meanwhile(2, halves)
        beside(0, other, 5, 12)
        for h in (0, 1):
            for k, dy in ((4, 0), (9, 3), (10, 1), (11, 2)):
                arrived(h, k, zh, dy, 1 - core, partner)
        meanwhile(3, halves)
        arrived(0, 7, other, 2, core, y_far)
        forward(0, 14)
        beside(1, other, 5, 12)
        meanwhile(4, halves)
        arrived(1, 7, other, 2, core, y_far)
        forward(1, 14)
        for h in (0, 1):
            for k, dy in ((8, 0), (12, 3), (13, 1), (14, 2)):
                arrived(h, k, other, dy, 1 - core, partner)

    def part_rows(p):
        return 48 * PARTS[p][0], 48 * (PARTS[p][1] - PARTS[p][0])

    def x_copy(it, h, k):
        size = part_rows((0, 1, 1, 0, 0, 1)[k])[1]
        return pltpu.make_async_remote_copy(
            src_ref=codes.at[h, k, 0:size, :], dst_ref=landed.at[it, h, k, 0:size, :],
            send_sem=x_send.at[it, h, k], recv_sem=x_recv.at[it, h, k],
            device_id=x_up if k % 2 == 0 else x_down, device_id_type=MESH,
        )

    def z_copy(it, h, d):
        return pltpu.make_async_remote_copy(
            src_ref=zcodes.at[h, (zl + d) % 4], dst_ref=zlanded.at[it, h, d - 1],
            send_sem=z_send.at[it, h, d - 1], recv_sem=z_recv.at[it, h, d - 1],
            device_id=z_peers[d - 1], device_id_type=MESH,
        )

    def multiply_near(n, halves):
        if n >= 3:
            halves(2 * n - 6, 2 * n - 4)

    def iteration(it, _):
        def multiply(n):
            product[n] = product[n] + jnp.dot(
                folded[(x + n) % 4, other], supply_of(it, other), preferred_element_type=f32
            )

        def code(h, k, n, landing=None):
            p = (0, 1, 1, 0, 0, 1)[k]
            first, size = part_rows(p)
            if landing is not None:
                x_copy(it, h, landing).wait_recv()

            def some(i, _):
                start = pl.multiple_of(i * 48, 16)
                value = product[n, pl.ds(first + start, 48), h * H : h * H + H]
                if landing is not None:
                    value = value + decode(landed[it, h, landing, pl.ds(start, 48), :])
                codes[h, k, pl.ds(start, 48), :] = encode(value)
                return 0

            lax.fori_loop(0, size // 48, some, 0)
            x_copy(it, h, k).start()

        def finish(h):
            for k in (2, 3, 4, 5):
                x_copy(it, h, k).wait_recv()
            for p, pair in enumerate(((3, 4), (2, 5))):
                for a in range(*PARTS[p]):
                    rows = slice(48 * (a - PARTS[p][0]), 48 * (a - PARTS[p][0]) + 48)
                    value = product[0, 48 * a : 48 * a + 48, h * H : h * H + H]
                    for k in pair:
                        value = value + decode(landed[it, h, k, rows, :])
                    for z in range(4):
                        flat[h, z, B * a : B * a + B, :] = value[B * z : B * z + B, :]
            for z in range(4):
                zcodes[h, z] = encode(flat[h, z])
            for d in (2, 1, 3):
                z_copy(it, h, d).start()

        multiply(2)
        code(0, 0, 2)
        code(0, 1, 2)
        send_halo(it)
        multiply(1)
        code(0, 2, 1)
        multiply(3)
        code(0, 3, 3)
        code(1, 0, 2)
        code(1, 1, 2)
        multiply(0)
        code(0, 4, 1, 0)
        code(0, 5, 3, 1)
        code(1, 2, 1)
        code(1, 3, 3)
        code(1, 4, 1, 0)
        code(1, 5, 3, 1)
        finish(0)
        finish(1)
        for copy in halo_copies(it):
            copy.wait_recv()
        for f, field in enumerate((tech, temp)):
            low = jnp.where(row == 0, 0.0, halo_in[it, 0, f, 0:B, :])
            high = jnp.where(row == 15, 0.0, halo_in[it, 1, f, 0:B, :])
            for a in range(A):
                padded[f, a, 1 : 1 + B, :] = field[a]
                padded[f, a, 0:1, :] = jnp.where(col == 0, 0.0, halo_in[it, 2, f, a : a + 1, :])
                padded[f, a, B + 1 : B + 2, :] = jnp.where(col == 15, 0.0, halo_in[it, 3, f, a : a + 1, :])
            for a in range(A):
                centre = field[a]
                below_ = low if a == 0 else padded[f, a - 1, 1 : 1 + B, :]
                above_ = high if a == A - 1 else padded[f, a + 1, 1 : 1 + B, :]
                lap = above_ + below_ + padded[f, a, 2 : 2 + B, :] + padded[f, a, 0:B, :] - 4.0 * centre
                tech_new[f, a] = centre + 0.2 * lap
        for a in range(A):
            tech_new[0, a] = tech_new[0, a] - 0.05 * temp[a] * temp[a]

        for h in (0, 1):
            for d in (1, 3, 2):
                z_copy(it, h, d).wait_recv()
            lanes = slice(h * H, h * H + H)
            total = flat[h, zl]
            for d in (1, 2, 3):
                total = total + decode(zlanded[it, h, d - 1])
            for a in range(A):
                target_ = 0.5 * (jnp.log(total[B * a : B * a + B, :]) + tech[a, :, lanes])
                wage_a = wage[a, :, lanes] + damping[0] * (target_ - wage[a, :, lanes])
                wage[a, :, lanes] = wage_a
                temp[a, :, lanes] = tech_new[1, a, :, lanes] + 0.5 * share[a, :, lanes] * jnp.tanh(wage_a)
                tech[a, :, lanes] = tech_new[0, a, :, lanes]

            @pl.when(it < ITERS - 1)
            def _():
                send_supply(it + 1, h)

        for copy in halo_copies(it):
            copy.wait_send()
        for h in (0, 1):
            for copy in gather_copies(it, h):
                copy().wait_send()
            for k in range(6):
                x_copy(it, h, k).wait_send()
            for d in (1, 2, 3):
                z_copy(it, h, d).wait_send()

        @pl.when(it < ITERS - 1)
        def _():
            gather(it + 1, multiply_near)

        return 0

    def build(n, halves):
        if n < 4:
            fold(n)
        else:
            halves(0, 4)

    pl.semaphore_wait(barrier, len(peers))
    for copy in starts:
        copy.wait()
    send_supply(0, 0)
    send_supply(0, 1)
    gather(0, build)
    lax.fori_loop(0, ITERS, iteration, 0)


def hand_on(*refs):
    for source, result in zip(refs[:3], refs[3:]):
        result[...] = source[...]


def local(cost_rough, land_mask, wage_start, tech_start, temp_start, damping):
    field = jax.ShapeDtypeStruct((A, B, S), f32)
    vmem = pl.BlockSpec(memory_space=pltpu.VMEM)
    hbm = pl.BlockSpec(memory_space=pl.ANY)
    dma = pltpu.SemaphoreType.DMA
    fields = pl.pallas_call(
        kernel,
        out_shape=(field, field, field),
        in_specs=[hbm, vmem, hbm, hbm, hbm, pl.BlockSpec(memory_space=pltpu.SMEM)],
        out_specs=(vmem, vmem, vmem),
        scratch_shapes=[
            pltpu.VMEM((A, LON, K), jnp.bfloat16),
            pltpu.VMEM((4, BLOCK, K), jnp.bfloat16),
            pltpu.VMEM((LON, K), f32),
            pltpu.VMEM((2, 16 * PIECE, 16 * PIECE), jnp.bfloat16),
            pltpu.VMEM((4, 2, BLOCK, WIDE), jnp.bfloat16),
            pltpu.VMEM((A, B, S), f32),
            pltpu.VMEM((ITERS, 2, 2, 3, SIDE, H), jnp.bfloat16),
            pltpu.VMEM((2, 3, PIECE, H), f32),
            pltpu.VMEM((4, BLOCK, S), f32),
            pltpu.VMEM((2, 6, 288, H), jnp.int16),
            pltpu.VMEM((ITERS, 2, 6, 288, H), jnp.int16),
            pltpu.VMEM((2, 4, FLAT, H), f32),
            pltpu.VMEM((2, 4, FLAT, H), jnp.int16),
            pltpu.VMEM((ITERS, 2, 3, FLAT, H), jnp.int16),
            pltpu.VMEM((2, A, 16, S), f32),
            pltpu.VMEM((ITERS, 4, 2, 16, S), f32),
            pltpu.VMEM((ITERS, 4, 2, 16, S), f32),
            pltpu.VMEM((2, A, B, S), f32),
            dma((3,)),
            dma((A,)),
            dma((ITERS, 2, 15)), dma((ITERS, 2, 15)),
            dma((ITERS, 2, 6)), dma((ITERS, 2, 6)),
            dma((ITERS, 2, 3)), dma((ITERS, 2, 3)),
            dma((ITERS, 4)), dma((ITERS, 4)),
        ],
        compiler_params=pltpu.CompilerParams(collective_id=0, has_side_effects=True, vmem_limit_bytes=60 * 1024 * 1024),
    )(cost_rough, land_mask, wage_start, tech_start, temp_start, damping)
    return pl.pallas_call(hand_on, out_shape=(field, field, field), in_specs=[vmem] * 3, out_specs=(vmem,) * 3)(*fields)


def solution(mesh):
    in_specs = (
        P("row", "col"),
        P("row", "col"),
        P("row", "col", None),
        P("row", "col", None),
        P("row", "col", None),
        P(),
    )
    out_specs = (P("row", "col", None), P("row", "col", None), P("row", "col", None))
    return jax.shard_map(local, mesh=mesh, in_specs=in_specs, out_specs=out_specs, check_vma=False)
```

```python
import functools

import jax
import jax.numpy as jnp
from jax import lax
from jax.experimental import pallas as pl
from jax.experimental.pallas import tpu as pltpu
from jax.sharding import PartitionSpec as P

LAT = 176
LON = 192
ITERS = 3
ELL = 44
A = 11
B = 12
S = 256
H = 128
BLOCK = 528
K = 2112
PIECE = 48
SIDE = 8 * PIECE
WIDE = 3 * SIDE
WINDOWS = ((0, 768, 0), (640, 768, 64), (1408, 704, 0))
PARTS = ((0, 6), (6, 11))
FLAT = 144
MESH = pl.DeviceIdType.MESH
f32 = jnp.float32
STEPS = 1024.0
MIDDLE = 8192.0
LN2 = 0.6931471805599453


def encode(value):
    code = jnp.log(jnp.maximum(value, 1e-30)) * (STEPS / LN2) + MIDDLE
    return jnp.round(jnp.clip(code, -32767.0, 32767.0)).astype(jnp.int32).astype(jnp.int16)


def decode(code):
    return jnp.exp((code.astype(jnp.int32).astype(f32) - MIDDLE) * (LN2 / STEPS))


def kernel(
    rough, mask, wage0, tech0, temp0, damping,
    wage_out, tech_out, temp_out,
    wage, tech, temp, stage, cost, near, pick, folded, share, gathered, piece, product, codes, landed, flat, zcodes, zlanded,
    padded, halo_out, halo_in, tech_new,
    start_sem, stage_sem, ag_send, ag_recv, x_send, x_recv, z_send, z_recv, halo_send, halo_recv,
):
    row, col = lax.axis_index("row"), lax.axis_index("col")
    zh, y, core = row // 8, (row // 2) % 4, row % 2
    x, zl = col // 4, col % 4

    def at_row(zh_, y_, core_):
        return zh_ * 8 + (y_ % 4) * 2 + core_

    def at_col(x_, zl_):
        return (x_ % 4) * 4 + zl_ % 4

    partner = (at_row(zh, y, 1 - core), col)
    across = (at_row(1 - zh, y, core), col)
    y_up, y_down = (at_row(zh, y + 1, core), col), (at_row(zh, y + 3, core), col)
    x_up, x_down = (row, at_col(x + 1, zl)), (row, at_col(x + 3, zl))
    z_peers = [(row, at_col(x, zl + d)) for d in (1, 2, 3)]
    halo_peers = [((row + 1) % 16, col), ((row + 15) % 16, col), (row, (col + 1) % 16), (row, (col + 15) % 16)]
    y_far = (at_row(zh, y + 2, core), col)
    peers = [partner, across, y_up, y_down, y_far, x_up, x_down] + z_peers + halo_peers

    def load_rough(a):
        return pltpu.make_async_copy(rough.at[pl.ds(a * LON, LON), :], stage.at[a], stage_sem.at[a])

    for a in range(A):
        load_rough(a).start()
    barrier = pltpu.get_barrier_semaphore()
    for peer in peers:
        pl.semaphore_signal(barrier, inc=1, device_id=peer, device_id_type=MESH)
    starts = [
        pltpu.make_async_copy(source, field, start_sem.at[n])
        for n, (source, field) in enumerate(((wage0, wage), (tech0, tech), (temp0, temp)))
    ]
    for copy in starts:
        copy.start()
    piece[...] = jnp.zeros_like(piece)
    flat[...] = jnp.zeros_like(flat)
    halo_out[...] = jnp.zeros_like(halo_out)
    diagonal = lax.broadcasted_iota(jnp.int32, (B, B), 0) == lax.broadcasted_iota(jnp.int32, (B, B), 1)
    for a in range(A):
        line = jnp.broadcast_to(mask[a : a + 1, :].astype(f32), (B, B))
        stand = jnp.sum(jnp.where(diagonal, line, 0.0), axis=1, keepdims=True)
        share[a] = jnp.broadcast_to(0.25 + stand, (B, S))

    spot = lax.broadcasted_iota(jnp.int32, (1, 16 * PIECE), 1)
    device = jnp.zeros_like(spot)
    for r in range(1, 16):
        device = device + (spot >= PIECE * r).astype(jnp.int32)
    rest = spot - PIECE * device
    target = (rest & 3) * LAT + A * device + (rest >> 2)
    target = jnp.where(rest < 4 * A, target, -4096)

    def pick_rows(i, _):
        start = pl.multiple_of(i * 16, 16)
        rows = i * 16 + lax.broadcasted_iota(jnp.int32, (16, 16 * PIECE), 0)
        for n, shift in enumerate((0, 64)):
            pick[n, pl.ds(start, 16), :] = jnp.where(rows == target + shift, 1.0, 0.0).astype(jnp.bfloat16)
        return 0

    lax.fori_loop(0, PIECE, pick_rows, 0)

    column = lax.broadcasted_iota(jnp.int32, (1, K), 1)
    local_b = jnp.zeros_like(column)
    for b in range(1, B):
        local_b = local_b + (column >= LAT * b).astype(jnp.int32)
    source_a = column - LAT * local_b
    source_b = col * B + local_b

    def near_rows(i, _):
        start = pl.multiple_of(i * 16, 16)
        rows = i * 16 + lax.broadcasted_iota(jnp.int32, (16, K), 0)
        near[pl.ds(start, 16), :] = jnp.exp(jnp.abs(rows - source_b).astype(f32) * (-1.0 / ELL))
        return 0

    lax.fori_loop(0, LON // 16, near_rows, 0)

    def cost_latitude(a, _):
        load_rough(a).wait()
        lat = jnp.exp(jnp.abs(row * A + a - source_a).astype(f32) * (-1.0 / ELL)) * (1.0 / (ELL * ELL))

        def cost_rows(i, _):
            start = pl.multiple_of(i * 16, 16)
            put = pl.multiple_of(a * 48 + (i % 3) * 16, 16)
            value = stage[a, pl.ds(start, 16), :].astype(f32) * (lat * near[pl.ds(start, 16), :])
            cost[i // 3, pl.ds(put, 16), :] = value.astype(jnp.bfloat16)
            return 0

        return lax.fori_loop(0, LON // 16, cost_rows, 0)

    lax.fori_loop(0, A, cost_latitude, 0)

    def fold(n):
        for g, (first, count, shift) in enumerate(WINDOWS):
            block = jnp.dot(
                cost[n, :, first : first + count], pick[1 if shift else 0, 0:count, :], preferred_element_type=f32
            ).astype(jnp.bfloat16)
            folded[n, 0, :, g * SIDE : g * SIDE + SIDE] = block[:, 0:SIDE]
            folded[n, 1, :, g * SIDE : g * SIDE + SIDE] = block[:, SIDE : 2 * SIDE]

    def slot(it, h, zh_, y_, core_):
        start = pl.multiple_of(((y_ % 4) * 2 + core_) * PIECE, 16)
        return gathered.at[it, zh_, h, :, pl.ds(start, PIECE), :]

    def ag(it, h, k, ref, peer):
        return pltpu.make_async_remote_copy(
            src_ref=ref, dst_ref=ref, send_sem=ag_send.at[h, k], recv_sem=ag_recv.at[it % 2, h, k],
            device_id=peer, device_id_type=MESH,
        )

    other = 1 - zh

    def gather_copies(it, h):
        own, theirs = slot(it, h, zh, y, core), slot(it, h, other, y, core)
        table = [
            (0, own, across), (1, own, y_up), (2, own, y_down), (3, own, y_far), (4, own, partner),
            (5, theirs, y_up), (6, theirs, y_down), (7, theirs, y_far), (8, theirs, partner),
            (9, slot(it, h, zh, y + 3, core), partner), (10, slot(it, h, zh, y + 1, core), partner),
            (11, slot(it, h, zh, y + 2, core), partner),
            (12, slot(it, h, other, y + 3, core), partner), (13, slot(it, h, other, y + 1, core), partner),
            (14, slot(it, h, other, y + 2, core), partner),
        ]
        return [functools.partial(ag, it, h, *entry) for entry in table]

    def halo_copies(it):
        return [
            pltpu.make_async_remote_copy(
                src_ref=halo_out.at[it, d], dst_ref=halo_in.at[it, d],
                send_sem=halo_send.at[d], recv_sem=halo_recv.at[it % 2, d],
                device_id=peer, device_id_type=MESH,
            )
            for d, peer in enumerate(halo_peers)
        ]

    def send_supply(it, h):
        for a in range(A):
            lanes = slice(h * H, h * H + H)
            value = jnp.exp(tech[a, :, lanes] - wage[a, :, lanes]) * share[a, :, lanes]
            for g in range(3):
                piece[h, g, 4 * a : 4 * a + 4, :] = value[4 * g : 4 * g + 4, :]
        start = pl.multiple_of((y * 2 + core) * PIECE, 16)
        gathered[it, zh, h, :, pl.ds(start, PIECE), :] = piece[h].astype(jnp.bfloat16)
        for copy in gather_copies(it, h)[0:5]:
            copy().start()

    def send_halo(it):
        for f, field in enumerate((tech, temp)):
            halo_out[it, 0, f, 0:B, :] = field[A - 1]
            halo_out[it, 1, f, 0:B, :] = field[0]
            for a in range(A):
                halo_out[it, 2, f, a : a + 1, :] = field[a, B - 1 : B, :]
                halo_out[it, 3, f, a : a + 1, :] = field[a, 0:1, :]
        for copy in halo_copies(it):
            copy.start()

    def supply_of(it, side):
        return jnp.concatenate([gathered[it, side, h].reshape(WIDE, H) for h in (0, 1)], axis=1)

    def gather(it, meanwhile):
        copies = [gather_copies(it, h) for h in (0, 1)]

        def arrived(h, k, zh_, dy, core_, peer):
            ag(it, h, k, slot(it, h, zh_, y + dy, core_), peer).wait_recv()

        def forward(h, *ks):
            for k in ks:
                copies[h][k]().start()

        def beside(h, side, first, then):
            arrived(h, first, side, 3, core, y_down)
            forward(h, then)
            arrived(h, first + 1, side, 1, core, y_up)
            forward(h, then + 1)

        def near_half(n, _):
            product[n] = jnp.dot(folded[(x + n) % 4, zh], supply_of(it, zh), preferred_element_type=f32)
            return 0

        def halves(first, last):
            lax.fori_loop(first, last, near_half, 0)

        for h in (0, 1):
            meanwhile(h, halves)
            beside(h, zh, 1, 9)
            arrived(h, 0, other, 0, core, across)
            forward(h, 5, 6, 7, 8)
            arrived(h, 3, zh, 2, core, y_far)
            forward(h, 11)
        meanwhile(2, halves)
        beside(0, other, 5, 12)
        arrived(0, 7, other, 2, core, y_far)
        forward(0, 14)
        for h in (0, 1):
            for k, dy in ((4, 0), (9, 3), (10, 1), (11, 2)):
                arrived(h, k, zh, dy, 1 - core, partner)
        meanwhile(3, halves)
        beside(1, other, 5, 12)
        arrived(1, 7, other, 2, core, y_far)
        forward(1, 14)
        meanwhile(4, halves)
        for h in (0, 1):
            for k, dy in ((8, 0), (12, 3), (13, 1), (14, 2)):
                arrived(h, k, other, dy, 1 - core, partner)

    def part_rows(p):
        return 48 * PARTS[p][0], 48 * (PARTS[p][1] - PARTS[p][0])

    def x_copy(it, h, k):
        size = part_rows((0, 1, 1, 0, 0, 1)[k])[1]
        return pltpu.make_async_remote_copy(
            src_ref=codes.at[h, k, 0:size, :], dst_ref=landed.at[it, h, k, 0:size, :],
            send_sem=x_send.at[h, k], recv_sem=x_recv.at[it % 2, h, k],
            device_id=x_up if k % 2 == 0 else x_down, device_id_type=MESH,
        )

    def z_copy(it, h, d):
        return pltpu.make_async_remote_copy(
            src_ref=zcodes.at[h, (zl + d) % 4], dst_ref=zlanded.at[it, h, d - 1],
            send_sem=z_send.at[h, d - 1], recv_sem=z_recv.at[it % 2, h, d - 1],
            device_id=z_peers[d - 1], device_id_type=MESH,
        )

    def multiply_near(n, halves):
        if n == 3:
            halves(1, 4)

    def leave(h):
        lanes = pl.ds(h * H, H)
        return [
            pltpu.make_async_copy(field.at[:, :, lanes], result.at[:, :, lanes], stage_sem.at[3 * h + n])
            for n, (field, result) in enumerate(((wage, wage_out), (tech, tech_out), (temp, temp_out)))
        ]

    def iteration(it, _):
        def multiply(n, first=0, size=BLOCK):
            rows = slice(first, first + size)
            product[n, rows] = product[n, rows] + jnp.dot(
                folded[(x + n) % 4, other, rows], supply_of(it, other), preferred_element_type=f32
            )

        def code(h, k, n, landing=None):
            p = (0, 1, 1, 0, 0, 1)[k]
            first, size = part_rows(p)
            if landing is not None:
                x_copy(it, h, landing).wait_recv()

            def some(i, _):
                start = pl.multiple_of(i * 48, 16)
                value = product[n, pl.ds(first + start, 48), h * H : h * H + H]
                if landing is not None:
                    value = value + decode(landed[it, h, landing, pl.ds(start, 48), :])
                codes[h, k, pl.ds(start, 48), :] = encode(value)
                return 0

            lax.fori_loop(0, size // 48, some, 0)
            x_copy(it, h, k).start()

        def finish(h):
            for k in (2, 3, 4, 5):
                x_copy(it, h, k).wait_recv()
            for p, pair in enumerate(((3, 4), (2, 5))):
                for a in range(*PARTS[p]):
                    rows = slice(48 * (a - PARTS[p][0]), 48 * (a - PARTS[p][0]) + 48)
                    value = product[0, 48 * a : 48 * a + 48, h * H : h * H + H]
                    for k in pair:
                        value = value + decode(landed[it, h, k, rows, :])
                    for z in range(4):
                        flat[h, z, B * a : B * a + B, :] = value[B * z : B * z + B, :]
            for z in range(4):
                zcodes[h, z] = encode(flat[h, z])
            for d in (2, 1, 3):
                z_copy(it, h, d).start()

        multiply(2, *part_rows(0))
        code(0, 0, 2)
        multiply(2, *part_rows(1))
        code(0, 1, 2)
        send_halo(it)
        multiply(1)
        code(0, 2, 1)
        multiply(3)
        code(0, 3, 3)
        code(1, 0, 2)
        code(1, 1, 2)
        code(0, 4, 1, 0)
        code(0, 5, 3, 1)
        code(1, 2, 1)
        code(1, 3, 3)
        for side in (zh, other):
            value = jnp.dot(folded[x, side], supply_of(it, side), preferred_element_type=f32)
            product[0] = value if side is zh else product[0] + value
        code(1, 4, 1, 0)
        code(1, 5, 3, 1)
        finish(0)
        finish(1)
        for copy in halo_copies(it):
            copy.wait_recv()
        for f, field in enumerate((tech, temp)):
            low = jnp.where(row == 0, 0.0, halo_in[it, 0, f, 0:B, :])
            high = jnp.where(row == 15, 0.0, halo_in[it, 1, f, 0:B, :])
            for a in range(A):
                padded[f, a, 1 : 1 + B, :] = field[a]
                padded[f, a, 0:1, :] = jnp.where(col == 0, 0.0, halo_in[it, 2, f, a : a + 1, :])
                padded[f, a, B + 1 : B + 2, :] = jnp.where(col == 15, 0.0, halo_in[it, 3, f, a : a + 1, :])
            for a in range(A):
                centre = field[a]
                below_ = low if a == 0 else padded[f, a - 1, 1 : 1 + B, :]
                above_ = high if a == A - 1 else padded[f, a + 1, 1 : 1 + B, :]
                lap = above_ + below_ + padded[f, a, 2 : 2 + B, :] + padded[f, a, 0:B, :] - 4.0 * centre
                tech_new[f, a] = centre + 0.2 * lap
        for a in range(A):
            tech_new[0, a] = tech_new[0, a] - 0.05 * temp[a] * temp[a]

        for copy in halo_copies(it):
            copy.wait_send()
        for h in (0, 1):
            for copy in gather_copies(it, h):
                copy().wait_send()
            for k in range(6):
                x_copy(it, h, k).wait_send()
        for h in (0, 1):
            for d in (1, 3, 2):
                z_copy(it, h, d).wait_recv()
            lanes = slice(h * H, h * H + H)
            total = flat[h, zl]
            for d in (1, 2, 3):
                total = total + decode(zlanded[it, h, d - 1])
            for a in range(A):
                target_ = 0.5 * (jnp.log(total[B * a : B * a + B, :]) + tech[a, :, lanes])
                wage_a = wage[a, :, lanes] + damping[0] * (target_ - wage[a, :, lanes])
                wage[a, :, lanes] = wage_a
                temp[a, :, lanes] = tech_new[1, a, :, lanes] + 0.5 * share[a, :, lanes] * jnp.tanh(wage_a)
                tech[a, :, lanes] = tech_new[0, a, :, lanes]

            @pl.when(it < ITERS - 1)
            def _():
                send_supply(it + 1, h)

            @pl.when(it == ITERS - 1)
            def _():
                for copy in leave(h):
                    copy.start()

        for h in (0, 1):
            for d in (1, 2, 3):
                z_copy(it, h, d).wait_send()

        @pl.when(it < ITERS - 1)
        def _():
            gather(it + 1, multiply_near)

        return 0

    def build(n, halves):
        if n == 0:
            fold(0)
            fold(1)
        elif n < 3:
            fold(n + 1)
        elif n == 4:
            halves(1, 4)

    pl.semaphore_wait(barrier, len(peers))
    for copy in starts:
        copy.wait()
    send_supply(0, 0)
    send_supply(0, 1)
    gather(0, build)
    lax.fori_loop(0, ITERS, iteration, 0)
    for h in (0, 1):
        for copy in leave(h):
            copy.wait()


def hand_on(*refs):
    sources, results, held, (sem,) = refs[0:3], refs[3:6], refs[6:9], refs[9:]
    into = [pltpu.make_async_copy(sources[n], held[n], sem.at[0, n]) for n in range(3)]
    out = [pltpu.make_async_copy(held[n], results[n], sem.at[1, n]) for n in range(3)]
    for copy in into:
        copy.start()
    for n in range(3):
        into[n].wait()
        out[n].start()
    for copy in out:
        copy.wait()


def local(cost_rough, land_mask, wage_start, tech_start, temp_start, damping):
    field = jax.ShapeDtypeStruct((A, B, S), f32)
    vmem = pl.BlockSpec(memory_space=pltpu.VMEM)
    hbm = pl.BlockSpec(memory_space=pl.ANY)
    dma = pltpu.SemaphoreType.DMA
    fields = pl.pallas_call(
        kernel,
        out_shape=(field, field, field),
        in_specs=[hbm, vmem, hbm, hbm, hbm, pl.BlockSpec(memory_space=pltpu.SMEM)],
        out_specs=(hbm, hbm, hbm),
        scratch_shapes=[
            pltpu.VMEM((A, B, S), f32),
            pltpu.VMEM((A, B, S), f32),
            pltpu.VMEM((A, B, S), f32),
            pltpu.VMEM((A, LON, K), jnp.bfloat16),
            pltpu.VMEM((4, BLOCK, K), jnp.bfloat16),
            pltpu.VMEM((LON, K), f32),
            pltpu.VMEM((2, 16 * PIECE, 16 * PIECE), jnp.bfloat16),
            pltpu.VMEM((4, 2, BLOCK, WIDE), jnp.bfloat16),
            pltpu.VMEM((A, B, S), f32),
            pltpu.VMEM((ITERS, 2, 2, 3, SIDE, H), jnp.bfloat16),
            pltpu.VMEM((2, 3, PIECE, H), f32),
            pltpu.VMEM((4, BLOCK, S), f32),
            pltpu.VMEM((2, 6, 288, H), jnp.int16),
            pltpu.VMEM((ITERS, 2, 6, 288, H), jnp.int16),
            pltpu.VMEM((2, 4, FLAT, H), f32),
            pltpu.VMEM((2, 4, FLAT, H), jnp.int16),
            pltpu.VMEM((ITERS, 2, 3, FLAT, H), jnp.int16),
            pltpu.VMEM((2, A, 16, S), f32),
            pltpu.VMEM((ITERS, 4, 2, 16, S), f32),
            pltpu.VMEM((ITERS, 4, 2, 16, S), f32),
            pltpu.VMEM((2, A, B, S), f32),
            dma((3,)),
            dma((A,)),
            dma((2, 15)), dma((2, 2, 15)),
            dma((2, 6)), dma((2, 2, 6)),
            dma((2, 3)), dma((2, 2, 3)),
            dma((4,)), dma((2, 4)),
        ],
        compiler_params=pltpu.CompilerParams(collective_id=0, has_side_effects=True, vmem_limit_bytes=60 * 1024 * 1024),
    )(cost_rough, land_mask, wage_start, tech_start, temp_start, damping)
    return pl.pallas_call(
        hand_on,
        out_shape=(field, field, field),
        in_specs=[hbm] * 3,
        out_specs=(hbm,) * 3,
        scratch_shapes=[pltpu.VMEM((A, B, S), f32)] * 3 + [dma((2, 3))],
    )(*fields)


def solution(mesh):
    in_specs = (
        P("row", "col"),
        P("row", "col"),
        P("row", "col", None),
        P("row", "col", None),
        P("row", "col", None),
        P(),
    )
    out_specs = (P("row", "col", None), P("row", "col", None), P("row", "col", None))
    return jax.shard_map(local, mesh=mesh, in_specs=in_specs, out_specs=out_specs, check_vma=False)
```

```python
import functools

import jax
import jax.numpy as jnp
from jax import lax
from jax.experimental import pallas as pl
from jax.experimental.pallas import tpu as pltpu
from jax.sharding import PartitionSpec as P

LAT = 176
LON = 192
ITERS = 3
ELL = 44
A = 11
B = 12
S = 256
H = 128
BLOCK = 528
K = 2112
PIECE = 48
SIDE = 8 * PIECE
WIDE = 3 * SIDE
WINDOWS = ((0, 768, 0), (640, 768, 64), (1408, 704, 0))
PARTS = (((0, 6), (6, 11)), ((0, 5), (5, 11)))
FLAT = 144
MESH = pl.DeviceIdType.MESH
f32 = jnp.float32
STEPS = 1024.0
MIDDLE = 8192.0
LN2 = 0.6931471805599453


def encode(value):
    code = jnp.log(jnp.maximum(value, 1e-30)) * (STEPS / LN2) + MIDDLE
    return jnp.round(jnp.clip(code, -32767.0, 32767.0)).astype(jnp.int32).astype(jnp.int16)


def decode(code):
    return jnp.exp((code.astype(jnp.int32).astype(f32) - MIDDLE) * (LN2 / STEPS))


def kernel(
    rough, mask, wage0, tech0, temp0, damping,
    wage_out, tech_out, temp_out,
    wage, tech, temp, stage, cost, near, pick, folded, share, gathered, piece, product, codes, landed, flat, zcodes, zlanded,
    padded, halo_out, halo_in, tech_new,
    start_sem, stage_sem, ag_send, ag_recv, x_send, x_recv, z_send, z_recv, halo_send, halo_recv,
):
    row, col = lax.axis_index("row"), lax.axis_index("col")
    zh, y, core = row // 8, (row // 2) % 4, row % 2
    x, zl = col // 4, col % 4

    def at_row(zh_, y_, core_):
        return zh_ * 8 + (y_ % 4) * 2 + core_

    def at_col(x_, zl_):
        return (x_ % 4) * 4 + zl_ % 4

    partner = (at_row(zh, y, 1 - core), col)
    across = (at_row(1 - zh, y, core), col)
    y_up, y_down = (at_row(zh, y + 1, core), col), (at_row(zh, y + 3, core), col)
    x_up, x_down = (row, at_col(x + 1, zl)), (row, at_col(x + 3, zl))
    z_peers = [(row, at_col(x, zl + d)) for d in (1, 2, 3)]
    halo_peers = [((row + 1) % 16, col), ((row + 15) % 16, col), (row, (col + 1) % 16), (row, (col + 15) % 16)]
    y_far = (at_row(zh, y + 2, core), col)
    peers = [partner, across, y_up, y_down, y_far, x_up, x_down] + z_peers + halo_peers

    def load_rough(a):
        return pltpu.make_async_copy(rough.at[pl.ds(a * LON, LON), :], stage.at[a], stage_sem.at[a])

    for a in range(A):
        load_rough(a).start()
    barrier = pltpu.get_barrier_semaphore()
    for peer in peers:
        pl.semaphore_signal(barrier, inc=1, device_id=peer, device_id_type=MESH)
    starts = [
        pltpu.make_async_copy(source, field, start_sem.at[n])
        for n, (source, field) in enumerate(((wage0, wage), (tech0, tech), (temp0, temp)))
    ]
    for copy in starts:
        copy.start()
    piece[...] = jnp.zeros_like(piece)
    flat[...] = jnp.zeros_like(flat)
    halo_out[...] = jnp.zeros_like(halo_out)
    diagonal = lax.broadcasted_iota(jnp.int32, (B, B), 0) == lax.broadcasted_iota(jnp.int32, (B, B), 1)
    for a in range(A):
        line = jnp.broadcast_to(mask[a : a + 1, :].astype(f32), (B, B))
        stand = jnp.sum(jnp.where(diagonal, line, 0.0), axis=1, keepdims=True)
        share[a] = jnp.broadcast_to(0.25 + stand, (B, S))

    spot = lax.broadcasted_iota(jnp.int32, (1, 16 * PIECE), 1)
    device = jnp.zeros_like(spot)
    for r in range(1, 16):
        device = device + (spot >= PIECE * r).astype(jnp.int32)
    rest = spot - PIECE * device
    target = (rest & 3) * LAT + A * device + (rest >> 2)
    target = jnp.where(rest < 4 * A, target, -4096)

    def pick_rows(i, _):
        start = pl.multiple_of(i * 16, 16)
        rows = i * 16 + lax.broadcasted_iota(jnp.int32, (16, 16 * PIECE), 0)
        for n, shift in enumerate((0, 64)):
            pick[n, pl.ds(start, 16), :] = jnp.where(rows == target + shift, 1.0, 0.0).astype(jnp.bfloat16)
        return 0

    lax.fori_loop(0, PIECE, pick_rows, 0)

    column = lax.broadcasted_iota(jnp.int32, (1, K), 1)
    local_b = jnp.zeros_like(column)
    for b in range(1, B):
        local_b = local_b + (column >= LAT * b).astype(jnp.int32)
    source_a = column - LAT * local_b
    source_b = col * B + local_b

    def near_rows(i, _):
        start = pl.multiple_of(i * 16, 16)
        rows = i * 16 + lax.broadcasted_iota(jnp.int32, (16, K), 0)
        near[pl.ds(start, 16), :] = jnp.exp(jnp.abs(rows - source_b).astype(f32) * (-1.0 / ELL))
        return 0

    lax.fori_loop(0, LON // 16, near_rows, 0)

    def cost_latitude(a, _):
        load_rough(a).wait()
        lat = jnp.exp(jnp.abs(row * A + a - source_a).astype(f32) * (-1.0 / ELL)) * (1.0 / (ELL * ELL))

        def cost_rows(i, _):
            start = pl.multiple_of(i * 16, 16)
            put = pl.multiple_of(a * 48 + (i % 3) * 16, 16)
            value = stage[a, pl.ds(start, 16), :].astype(f32) * (lat * near[pl.ds(start, 16), :])
            cost[i // 3, pl.ds(put, 16), :] = value.astype(jnp.bfloat16)
            return 0

        return lax.fori_loop(0, LON // 16, cost_rows, 0)

    lax.fori_loop(0, A, cost_latitude, 0)

    def fold(n):
        for g, (first, count, shift) in enumerate(WINDOWS):
            block = jnp.dot(
                cost[n, :, first : first + count], pick[1 if shift else 0, 0:count, :], preferred_element_type=f32
            ).astype(jnp.bfloat16)
            folded[n, 0, :, g * SIDE : g * SIDE + SIDE] = block[:, 0:SIDE]
            folded[n, 1, :, g * SIDE : g * SIDE + SIDE] = block[:, SIDE : 2 * SIDE]

    def slot(it, h, zh_, y_, core_):
        start = pl.multiple_of(((y_ % 4) * 2 + core_) * PIECE, 16)
        return gathered.at[it, zh_, h, :, pl.ds(start, PIECE), :]

    def ag(it, h, k, ref, peer):
        return pltpu.make_async_remote_copy(
            src_ref=ref, dst_ref=ref, send_sem=ag_send.at[h, k], recv_sem=ag_recv.at[it % 2, h, k],
            device_id=peer, device_id_type=MESH,
        )

    other = 1 - zh

    def gather_copies(it, h):
        own, theirs = slot(it, h, zh, y, core), slot(it, h, other, y, core)
        table = [
            (0, own, across), (1, own, y_up), (2, own, y_down), (3, own, y_far), (4, own, partner),
            (5, theirs, y_up), (6, theirs, y_down), (7, theirs, y_far), (8, theirs, partner),
            (9, slot(it, h, zh, y + 3, core), partner), (10, slot(it, h, zh, y + 1, core), partner),
            (11, slot(it, h, zh, y + 2, core), partner),
            (12, slot(it, h, other, y + 3, core), partner), (13, slot(it, h, other, y + 1, core), partner),
            (14, slot(it, h, other, y + 2, core), partner),
        ]
        return [functools.partial(ag, it, h, *entry) for entry in table]

    def halo_copy(it, d):
        return pltpu.make_async_remote_copy(
            src_ref=halo_out.at[it, d], dst_ref=halo_in.at[it, d],
            send_sem=halo_send.at[d], recv_sem=halo_recv.at[it % 2, d],
            device_id=halo_peers[d], device_id_type=MESH,
        )

    def send_supply(it, h):
        for a in range(A):
            lanes = slice(h * H, h * H + H)
            value = jnp.exp(tech[a, :, lanes] - wage[a, :, lanes]) * share[a, :, lanes]
            for g in range(3):
                piece[h, g, 4 * a : 4 * a + 4, :] = value[4 * g : 4 * g + 4, :]
        start = pl.multiple_of((y * 2 + core) * PIECE, 16)
        gathered[it, zh, h, :, pl.ds(start, PIECE), :] = piece[h].astype(jnp.bfloat16)
        for copy in gather_copies(it, h)[0:5]:
            copy().start()

    def send_halo_rows(it):
        for f, field in enumerate((tech, temp)):
            halo_out[it, 0, f, 0:B, :] = field[A - 1]
            halo_out[it, 1, f, 0:B, :] = field[0]
        for d in (0, 1):
            halo_copy(it, d).start()

    def send_halo_columns(it):
        for f, field in enumerate((tech, temp)):
            for a in range(A):
                halo_out[it, 2, f, a : a + 1, :] = field[a, B - 1 : B, :]
                halo_out[it, 3, f, a : a + 1, :] = field[a, 0:1, :]
        for d in (2, 3):
            halo_copy(it, d).start()

    def supply_of(it, side):
        return jnp.concatenate([gathered[it, side, h].reshape(WIDE, H) for h in (0, 1)], axis=1)

    def gather(it, meanwhile):
        copies = [gather_copies(it, h) for h in (0, 1)]

        def arrived(h, k, zh_, dy, core_, peer):
            ag(it, h, k, slot(it, h, zh_, y + dy, core_), peer).wait_recv()

        def forward(h, *ks):
            for k in ks:
                copies[h][k]().start()

        def beside(h, side, first, then):
            arrived(h, first, side, 3, core, y_down)
            forward(h, then)
            arrived(h, first + 1, side, 1, core, y_up)
            forward(h, then + 1)

        def near_half(n, _):
            product[n] = jnp.dot(folded[(x + n) % 4, zh], supply_of(it, zh), preferred_element_type=f32)
            return 0

        def halves(first, last):
            lax.fori_loop(first, last, near_half, 0)

        for h in (0, 1):
            meanwhile(h, halves)
            beside(h, zh, 1, 9)
            arrived(h, 0, other, 0, core, across)
            forward(h, 5, 6, 7, 8)
            arrived(h, 3, zh, 2, core, y_far)
            forward(h, 11)
        send_halo_columns(it)
        meanwhile(2, halves)
        for h in (0, 1):
            for k, dy in ((4, 0), (9, 3), (10, 1), (11, 2)):
                arrived(h, k, zh, dy, 1 - core, partner)
        meanwhile(3, halves)
        beside(0, other, 5, 12)
        arrived(0, 7, other, 2, core, y_far)
        forward(0, 14)
        beside(1, other, 5, 12)
        arrived(1, 7, other, 2, core, y_far)
        forward(1, 14)
        meanwhile(4, halves)
        for h in (0, 1):
            for k, dy in ((8, 0), (12, 3), (13, 1), (14, 2)):
                arrived(h, k, other, dy, 1 - core, partner)

    def part_rows(h, p):
        first, last = PARTS[h][p]
        return 48 * first, 48 * (last - first)

    def x_copy(it, h, k):
        size = part_rows(h, (0, 1, 1, 0, 0, 1)[k])[1]
        return pltpu.make_async_remote_copy(
            src_ref=codes.at[h, k, 0:size, :], dst_ref=landed.at[it, h, k, 0:size, :],
            send_sem=x_send.at[h, k], recv_sem=x_recv.at[it % 2, h, k],
            device_id=x_up if k % 2 == 0 else x_down, device_id_type=MESH,
        )

    def z_copy(it, h, d):
        return pltpu.make_async_remote_copy(
            src_ref=zcodes.at[h, (zl + d) % 4], dst_ref=zlanded.at[it, h, d - 1],
            send_sem=z_send.at[h, d - 1], recv_sem=z_recv.at[it % 2, h, d - 1],
            device_id=z_peers[d - 1], device_id_type=MESH,
        )

    def multiply_near(n, halves):
        if n == 3:
            halves(1, 3)

    def leave(h):
        lanes = pl.ds(h * H, H)
        return [
            pltpu.make_async_copy(field.at[:, :, lanes], result.at[:, :, lanes], stage_sem.at[3 * h + n])
            for n, (field, result) in enumerate(((wage, wage_out), (tech, tech_out), (temp, temp_out)))
        ]

    def iteration(it, _):
        def multiply(n, first=0, size=BLOCK):
            rows = slice(first, first + size)
            product[n, rows] = product[n, rows] + jnp.dot(
                folded[(x + n) % 4, other, rows], supply_of(it, other), preferred_element_type=f32
            )

        def code(h, k, n, landing=None):
            p = (0, 1, 1, 0, 0, 1)[k]
            first, size = part_rows(h, p)
            if landing is not None:
                x_copy(it, h, landing).wait_recv()

            def some(i, _):
                start = pl.multiple_of(i * 48, 16)
                value = product[n, pl.ds(first + start, 48), h * H : h * H + H]
                if landing is not None:
                    value = value + decode(landed[it, h, landing, pl.ds(start, 48), :])
                codes[h, k, pl.ds(start, 48), :] = encode(value)
                return 0

            lax.fori_loop(0, size // 48, some, 0)
            x_copy(it, h, k).start()

        def finish(h):
            for k in (2, 3, 4, 5):
                x_copy(it, h, k).wait_recv()
            for p, pair in enumerate(((3, 4), (2, 5))):
                for a in range(*PARTS[h][p]):
                    rows = slice(48 * (a - PARTS[h][p][0]), 48 * (a - PARTS[h][p][0]) + 48)
                    value = product[0, 48 * a : 48 * a + 48, h * H : h * H + H]
                    for k in pair:
                        value = value + decode(landed[it, h, k, rows, :])
                    for z in range(4):
                        flat[h, z, B * a : B * a + B, :] = value[B * z : B * z + B, :]
            for z in range(4):
                zcodes[h, z] = encode(flat[h, z])
            for d in (2, 1, 3):
                z_copy(it, h, d).start()

        def multiply_whole(n):
            for side in (zh, other):
                value = jnp.dot(folded[(x + n) % 4, side], supply_of(it, side), preferred_element_type=f32)
                product[n] = value if side is zh else product[n] + value

        multiply(2, *part_rows(0, 0))
        code(0, 0, 2)
        multiply(2, *part_rows(0, 1))
        code(0, 1, 2)
        send_halo_rows(it)
        multiply(1)
        code(0, 2, 1)
        code(1, 1, 2)
        multiply_whole(3)
        code(0, 3, 3)
        code(1, 0, 2)
        code(0, 4, 1, 0)
        code(0, 5, 3, 1)
        code(1, 2, 1)
        code(1, 3, 3)
        multiply_whole(0)
        code(1, 4, 1, 0)
        code(1, 5, 3, 1)
        finish(0)
        finish(1)
        for d in range(4):
            halo_copy(it, d).wait_recv()
        for f, field in enumerate((tech, temp)):
            low = jnp.where(row == 0, 0.0, halo_in[it, 0, f, 0:B, :])
            high = jnp.where(row == 15, 0.0, halo_in[it, 1, f, 0:B, :])
            for a in range(A):
                padded[f, a, 1 : 1 + B, :] = field[a]
                padded[f, a, 0:1, :] = jnp.where(col == 0, 0.0, halo_in[it, 2, f, a : a + 1, :])
                padded[f, a, B + 1 : B + 2, :] = jnp.where(col == 15, 0.0, halo_in[it, 3, f, a : a + 1, :])
            for a in range(A):
                centre = field[a]
                below_ = low if a == 0 else padded[f, a - 1, 1 : 1 + B, :]
                above_ = high if a == A - 1 else padded[f, a + 1, 1 : 1 + B, :]
                lap = above_ + below_ + padded[f, a, 2 : 2 + B, :] + padded[f, a, 0:B, :] - 4.0 * centre
                tech_new[f, a] = centre + 0.2 * lap
        for a in range(A):
            tech_new[0, a] = tech_new[0, a] - 0.05 * temp[a] * temp[a]

        for d in range(4):
            halo_copy(it, d).wait_send()
        for h in (0, 1):
            for copy in gather_copies(it, h):
                copy().wait_send()
            for k in range(6):
                x_copy(it, h, k).wait_send()
        for h in (0, 1):
            for d in (1, 3, 2):
                z_copy(it, h, d).wait_recv()
            lanes = slice(h * H, h * H + H)
            total = flat[h, zl]
            for d in (1, 2, 3):
                total = total + decode(zlanded[it, h, d - 1])
            for a in range(A):
                target_ = 0.5 * (jnp.log(total[B * a : B * a + B, :]) + tech[a, :, lanes])
                wage_a = wage[a, :, lanes] + damping[0] * (target_ - wage[a, :, lanes])
                wage[a, :, lanes] = wage_a
                temp[a, :, lanes] = tech_new[1, a, :, lanes] + 0.5 * share[a, :, lanes] * jnp.tanh(wage_a)
                tech[a, :, lanes] = tech_new[0, a, :, lanes]

            @pl.when(it < ITERS - 1)
            def _():
                send_supply(it + 1, h)

            @pl.when(it == ITERS - 1)
            def _():
                for copy in leave(h):
                    copy.start()

        for h in (0, 1):
            for d in (1, 2, 3):
                z_copy(it, h, d).wait_send()

        @pl.when(it < ITERS - 1)
        def _():
            gather(it + 1, multiply_near)

        return 0

    def build(n, halves):
        if n == 0:
            fold(0)
            fold(1)
        elif n == 2:
            fold(2)
            fold(3)
        elif n == 4:
            halves(1, 3)

    pl.semaphore_wait(barrier, len(peers))
    for copy in starts:
        copy.wait()
    send_supply(0, 0)
    send_supply(0, 1)
    gather(0, build)
    lax.fori_loop(0, ITERS, iteration, 0)
    for h in (0, 1):
        for copy in leave(h):
            copy.wait()


def hand_on(*refs):
    sources, results, held, (sem,) = refs[0:3], refs[3:6], refs[6:9], refs[9:]
    into = [pltpu.make_async_copy(sources[n], held[n], sem.at[0, n]) for n in range(3)]
    out = [pltpu.make_async_copy(held[n], results[n], sem.at[1, n]) for n in range(3)]
    for copy in into:
        copy.start()
    for n in range(3):
        into[n].wait()
        out[n].start()
    for copy in out:
        copy.wait()


def local(cost_rough, land_mask, wage_start, tech_start, temp_start, damping):
    field = jax.ShapeDtypeStruct((A, B, S), f32)
    vmem = pl.BlockSpec(memory_space=pltpu.VMEM)
    hbm = pl.BlockSpec(memory_space=pl.ANY)
    dma = pltpu.SemaphoreType.DMA
    fields = pl.pallas_call(
        kernel,
        out_shape=(field, field, field),
        in_specs=[hbm, vmem, hbm, hbm, hbm, pl.BlockSpec(memory_space=pltpu.SMEM)],
        out_specs=(hbm, hbm, hbm),
        scratch_shapes=[
            pltpu.VMEM((A, B, S), f32),
            pltpu.VMEM((A, B, S), f32),
            pltpu.VMEM((A, B, S), f32),
            pltpu.VMEM((A, LON, K), jnp.bfloat16),
            pltpu.VMEM((4, BLOCK, K), jnp.bfloat16),
            pltpu.VMEM((LON, K), f32),
            pltpu.VMEM((2, 16 * PIECE, 16 * PIECE), jnp.bfloat16),
            pltpu.VMEM((4, 2, BLOCK, WIDE), jnp.bfloat16),
            pltpu.VMEM((A, B, S), f32),
            pltpu.VMEM((ITERS, 2, 2, 3, SIDE, H), jnp.bfloat16),
            pltpu.VMEM((2, 3, PIECE, H), f32),
            pltpu.VMEM((4, BLOCK, S), f32),
            pltpu.VMEM((2, 6, 288, H), jnp.int16),
            pltpu.VMEM((ITERS, 2, 6, 288, H), jnp.int16),
            pltpu.VMEM((2, 4, FLAT, H), f32),
            pltpu.VMEM((2, 4, FLAT, H), jnp.int16),
            pltpu.VMEM((ITERS, 2, 3, FLAT, H), jnp.int16),
            pltpu.VMEM((2, A, 16, S), f32),
            pltpu.VMEM((ITERS, 4, 2, 16, S), f32),
            pltpu.VMEM((ITERS, 4, 2, 16, S), f32),
            pltpu.VMEM((2, A, B, S), f32),
            dma((3,)),
            dma((A,)),
            dma((2, 15)), dma((2, 2, 15)),
            dma((2, 6)), dma((2, 2, 6)),
            dma((2, 3)), dma((2, 2, 3)),
            dma((4,)), dma((2, 4)),
        ],
        compiler_params=pltpu.CompilerParams(collective_id=0, has_side_effects=True, vmem_limit_bytes=60 * 1024 * 1024),
    )(cost_rough, land_mask, wage_start, tech_start, temp_start, damping)
    return pl.pallas_call(
        hand_on,
        out_shape=(field, field, field),
        in_specs=[hbm] * 3,
        out_specs=(hbm,) * 3,
        scratch_shapes=[pltpu.VMEM((A, B, S), f32)] * 3 + [dma((2, 3))],
    )(*fields)


def solution(mesh):
    in_specs = (
        P("row", "col"),
        P("row", "col"),
        P("row", "col", None),
        P("row", "col", None),
        P("row", "col", None),
        P(),
    )
    out_specs = (P("row", "col", None), P("row", "col", None), P("row", "col", None))
    return jax.shard_map(local, mesh=mesh, in_specs=in_specs, out_specs=out_specs, check_vma=False)
```

```python
import functools

import jax
import jax.numpy as jnp
from jax import lax
from jax.experimental import pallas as pl
from jax.experimental.pallas import tpu as pltpu
from jax.sharding import PartitionSpec as P

LAT = 176
LON = 192
ITERS = 3
ELL = 44
A = 11
B = 12
S = 256
H = 128
BLOCK = 528
K = 2112
PIECE = 48
SIDE = 8 * PIECE
WIDE = 3 * SIDE
WINDOWS = ((0, 768, 0), (640, 768, 64), (1408, 704, 0))
PARTS = (((0, 6), (6, 11)), ((0, 5), (5, 11)))
FLAT = 144
FLAT_ROWS = (slice(0, 80), slice(80, 144))
MESH = pl.DeviceIdType.MESH
f32 = jnp.float32
STEPS = 1024.0
MIDDLE = 8192.0
LN2 = 0.6931471805599453


def encode(value):
    code = jnp.log(jnp.maximum(value, 1e-30)) * (STEPS / LN2) + MIDDLE
    return jnp.round(jnp.clip(code, -32767.0, 32767.0)).astype(jnp.int32).astype(jnp.int16)


def decode(code):
    return jnp.exp((code.astype(jnp.int32).astype(f32) - MIDDLE) * (LN2 / STEPS))


def kernel(
    rough, mask, wage0, tech0, temp0, damping,
    wage_out, tech_out, temp_out,
    wage, tech, temp, stage, cost, near, pick, folded, share, gathered, piece, product, codes, landed, flat, zcodes, zlanded,
    padded, halo_out, halo_in, tech_new,
    start_sem, stage_sem, ag_send, ag_recv, x_send, x_recv, z_send, z_recv, halo_send, halo_recv,
):
    row, col = lax.axis_index("row"), lax.axis_index("col")
    zh, y, core = row // 8, (row // 2) % 4, row % 2
    x, zl = col // 4, col % 4

    def at_row(zh_, y_, core_):
        return zh_ * 8 + (y_ % 4) * 2 + core_

    def at_col(x_, zl_):
        return (x_ % 4) * 4 + zl_ % 4

    partner = (at_row(zh, y, 1 - core), col)
    across = (at_row(1 - zh, y, core), col)
    y_up, y_down = (at_row(zh, y + 1, core), col), (at_row(zh, y + 3, core), col)
    x_up, x_down = (row, at_col(x + 1, zl)), (row, at_col(x + 3, zl))
    z_peers = [(row, at_col(x, zl + d)) for d in (1, 2, 3)]
    halo_peers = [((row + 1) % 16, col), ((row + 15) % 16, col), (row, (col + 1) % 16), (row, (col + 15) % 16)]
    y_far = (at_row(zh, y + 2, core), col)
    peers = [partner, across, y_up, y_down, y_far, x_up, x_down] + z_peers + halo_peers

    def load_rough(a):
        return pltpu.make_async_copy(rough.at[pl.ds(a * LON, LON), :], stage.at[a], stage_sem.at[a])

    for a in range(A):
        load_rough(a).start()
    barrier = pltpu.get_barrier_semaphore()
    for peer in peers:
        pl.semaphore_signal(barrier, inc=1, device_id=peer, device_id_type=MESH)
    starts = [
        pltpu.make_async_copy(source, field, start_sem.at[n])
        for n, (source, field) in enumerate(((wage0, wage), (tech0, tech), (temp0, temp)))
    ]
    for copy in starts:
        copy.start()
    piece[...] = jnp.zeros_like(piece)
    flat[...] = jnp.zeros_like(flat)
    halo_out[...] = jnp.zeros_like(halo_out)
    diagonal = lax.broadcasted_iota(jnp.int32, (B, B), 0) == lax.broadcasted_iota(jnp.int32, (B, B), 1)
    for a in range(A):
        line = jnp.broadcast_to(mask[a : a + 1, :].astype(f32), (B, B))
        stand = jnp.sum(jnp.where(diagonal, line, 0.0), axis=1, keepdims=True)
        share[a] = jnp.broadcast_to(0.25 + stand, (B, S))

    spot = lax.broadcasted_iota(jnp.int32, (1, 16 * PIECE), 1)
    device = jnp.zeros_like(spot)
    for r in range(1, 16):
        device = device + (spot >= PIECE * r).astype(jnp.int32)
    rest = spot - PIECE * device
    target = (rest & 3) * LAT + A * device + (rest >> 2)
    target = jnp.where(rest < 4 * A, target, -4096)

    def pick_rows(i, _):
        start = pl.multiple_of(i * 16, 16)
        rows = i * 16 + lax.broadcasted_iota(jnp.int32, (16, 16 * PIECE), 0)
        for n, shift in enumerate((0, 64)):
            pick[n, pl.ds(start, 16), :] = jnp.where(rows == target + shift, 1.0, 0.0).astype(jnp.bfloat16)
        return 0

    lax.fori_loop(0, PIECE, pick_rows, 0)

    column = lax.broadcasted_iota(jnp.int32, (1, K), 1)
    local_b = jnp.zeros_like(column)
    for b in range(1, B):
        local_b = local_b + (column >= LAT * b).astype(jnp.int32)
    source_a = column - LAT * local_b
    source_b = col * B + local_b

    def near_rows(i, _):
        start = pl.multiple_of(i * 16, 16)
        rows = i * 16 + lax.broadcasted_iota(jnp.int32, (16, K), 0)
        near[pl.ds(start, 16), :] = jnp.exp(jnp.abs(rows - source_b).astype(f32) * (-1.0 / ELL))
        return 0

    lax.fori_loop(0, LON // 16, near_rows, 0)

    def cost_latitude(a, _):
        load_rough(a).wait()
        lat = jnp.exp(jnp.abs(row * A + a - source_a).astype(f32) * (-1.0 / ELL)) * (1.0 / (ELL * ELL))

        def cost_rows(i, _):
            start = pl.multiple_of(i * 16, 16)
            put = pl.multiple_of(a * 48 + (i % 3) * 16, 16)
            value = stage[a, pl.ds(start, 16), :].astype(f32) * (lat * near[pl.ds(start, 16), :])
            cost[i // 3, pl.ds(put, 16), :] = value.astype(jnp.bfloat16)
            return 0

        return lax.fori_loop(0, LON // 16, cost_rows, 0)

    lax.fori_loop(0, A, cost_latitude, 0)

    def fold(n):
        for g, (first, count, shift) in enumerate(WINDOWS):
            block = jnp.dot(
                cost[n, :, first : first + count], pick[1 if shift else 0, 0:count, :], preferred_element_type=f32
            ).astype(jnp.bfloat16)
            folded[n, 0, :, g * SIDE : g * SIDE + SIDE] = block[:, 0:SIDE]
            folded[n, 1, :, g * SIDE : g * SIDE + SIDE] = block[:, SIDE : 2 * SIDE]

    def slot(it, h, zh_, y_, core_):
        start = pl.multiple_of(((y_ % 4) * 2 + core_) * PIECE, 16)
        return gathered.at[it, zh_, h, :, pl.ds(start, PIECE), :]

    def ag(it, h, k, ref, peer):
        return pltpu.make_async_remote_copy(
            src_ref=ref, dst_ref=ref, send_sem=ag_send.at[h, k], recv_sem=ag_recv.at[it % 2, h, k],
            device_id=peer, device_id_type=MESH,
        )

    other = 1 - zh

    def gather_copies(it, h):
        own, theirs = slot(it, h, zh, y, core), slot(it, h, other, y, core)
        table = [
            (0, own, across), (1, own, y_up), (2, own, y_down), (3, own, y_far), (4, own, partner),
            (5, theirs, y_up), (6, theirs, y_down), (7, theirs, y_far), (8, theirs, partner),
            (9, slot(it, h, zh, y + 3, core), partner), (10, slot(it, h, zh, y + 1, core), partner),
            (11, slot(it, h, zh, y + 2, core), partner),
            (12, slot(it, h, other, y + 3, core), partner), (13, slot(it, h, other, y + 1, core), partner),
            (14, slot(it, h, other, y + 2, core), partner),
        ]
        return [functools.partial(ag, it, h, *entry) for entry in table]

    def halo_copy(it, d):
        return pltpu.make_async_remote_copy(
            src_ref=halo_out.at[it, d], dst_ref=halo_in.at[it, d],
            send_sem=halo_send.at[d], recv_sem=halo_recv.at[it % 2, d],
            device_id=halo_peers[d], device_id_type=MESH,
        )

    def send_supply(it, h):
        for a in range(A):
            lanes = slice(h * H, h * H + H)
            value = jnp.exp(tech[a, :, lanes] - wage[a, :, lanes]) * share[a, :, lanes]
            for g in range(3):
                piece[h, g, 4 * a : 4 * a + 4, :] = value[4 * g : 4 * g + 4, :]
        start = pl.multiple_of((y * 2 + core) * PIECE, 16)
        gathered[it, zh, h, :, pl.ds(start, PIECE), :] = piece[h].astype(jnp.bfloat16)
        for copy in gather_copies(it, h)[0:5]:
            copy().start()

    def send_halo_rows(it):
        for f, field in enumerate((tech, temp)):
            halo_out[it, 0, f, 0:B, :] = field[A - 1]
            halo_out[it, 1, f, 0:B, :] = field[0]
        for d in (0, 1):
            halo_copy(it, d).start()

    def send_halo_columns(it):
        for f, field in enumerate((tech, temp)):
            for a in range(A):
                halo_out[it, 2, f, a : a + 1, :] = field[a, B - 1 : B, :]
                halo_out[it, 3, f, a : a + 1, :] = field[a, 0:1, :]
        for d in (2, 3):
            halo_copy(it, d).start()

    def supply_of(it, side):
        return jnp.concatenate([gathered[it, side, h].reshape(WIDE, H) for h in (0, 1)], axis=1)

    def gather(it, meanwhile):
        copies = [gather_copies(it, h) for h in (0, 1)]

        def arrived(h, k, zh_, dy, core_, peer):
            ag(it, h, k, slot(it, h, zh_, y + dy, core_), peer).wait_recv()

        def forward(h, *ks):
            for k in ks:
                copies[h][k]().start()

        def beside(h, side, first, then):
            arrived(h, first, side, 3, core, y_down)
            forward(h, then)
            arrived(h, first + 1, side, 1, core, y_up)
            forward(h, then + 1)

        def near_half(n, _):
            product[n] = jnp.dot(folded[(x + n) % 4, zh], supply_of(it, zh), preferred_element_type=f32)
            return 0

        def halves(first, last):
            lax.fori_loop(first, last, near_half, 0)

        for h in (0, 1):
            meanwhile(h, halves)
            beside(h, zh, 1, 9)
            arrived(h, 0, other, 0, core, across)
            forward(h, 5, 6, 7, 8)
            arrived(h, 3, zh, 2, core, y_far)
            forward(h, 11)
        send_halo_columns(it)
        meanwhile(2, halves)
        for h in (0, 1):
            for k, dy in ((4, 0), (9, 3), (10, 1), (11, 2)):
                arrived(h, k, zh, dy, 1 - core, partner)
        meanwhile(3, halves)
        beside(0, other, 5, 12)
        arrived(0, 7, other, 2, core, y_far)
        forward(0, 14)
        beside(1, other, 5, 12)
        arrived(1, 7, other, 2, core, y_far)
        forward(1, 14)
        meanwhile(4, halves)
        for h in (0, 1):
            for k, dy in ((8, 0), (12, 3), (13, 1), (14, 2)):
                arrived(h, k, other, dy, 1 - core, partner)

    def part_rows(h, p):
        first, last = PARTS[h][p]
        return 48 * first, 48 * (last - first)

    def piece_of(h, p, s):
        first, last = PARTS[h][p]
        middle = first + (last - first + 1) // 2
        return ((first, middle), (middle, last))[s]

    def places(h, s):
        latitudes = [a for p in (0, 1) for a in range(*piece_of(h, p, s))]
        return {a: FLAT_ROWS[s].start + B * n for n, a in enumerate(latitudes)}

    def x_rows(h, k, s):
        p = (0, 1, 1, 0, 0, 1)[k]
        first, last = PARTS[h][p] if s is None else piece_of(h, p, s)
        return 48 * (first - PARTS[h][p][0]), 48 * (last - first)

    def x_copy(it, h, k, s=None):
        first, size = x_rows(h, k, s)
        sem = k if s is None else 2 * k - 4 + s
        return pltpu.make_async_remote_copy(
            src_ref=codes.at[h, k, pl.ds(first, size), :], dst_ref=landed.at[it, h, k, pl.ds(first, size), :],
            send_sem=x_send.at[h, sem], recv_sem=x_recv.at[it % 2, h, sem],
            device_id=x_up if k % 2 == 0 else x_down, device_id_type=MESH,
        )

    def x_copies(it, h):
        return [x_copy(it, h, k) for k in range(4)] + [x_copy(it, h, k, s) for k in (4, 5) for s in (0, 1)]

    def z_copy(it, h, s, d):
        rows = pl.ds(FLAT_ROWS[s].start, FLAT_ROWS[s].stop - FLAT_ROWS[s].start)
        return pltpu.make_async_remote_copy(
            src_ref=zcodes.at[h, (zl + d) % 4, rows, :], dst_ref=zlanded.at[it, h, d - 1, rows, :],
            send_sem=z_send.at[h, s, d - 1], recv_sem=z_recv.at[it % 2, h, s, d - 1],
            device_id=z_peers[d - 1], device_id_type=MESH,
        )

    def multiply_near(n, halves):
        if n == 3:
            halves(1, 3)

    def leave(h):
        lanes = pl.ds(h * H, H)
        return [
            pltpu.make_async_copy(field.at[:, :, lanes], result.at[:, :, lanes], stage_sem.at[3 * h + n])
            for n, (field, result) in enumerate(((wage, wage_out), (tech, tech_out), (temp, temp_out)))
        ]

    def iteration(it, _):
        def multiply(n, first=0, size=BLOCK):
            rows = slice(first, first + size)
            product[n, rows] = product[n, rows] + jnp.dot(
                folded[(x + n) % 4, other, rows], supply_of(it, other), preferred_element_type=f32
            )

        def code(h, k, n, landing=None, s=None):
            base = 48 * PARTS[h][(0, 1, 1, 0, 0, 1)[k]][0]
            first, size = x_rows(h, k, s)

            def some(i, _):
                start = pl.multiple_of(first + i * 48, 16)
                value = product[n, pl.ds(base + start, 48), h * H : h * H + H]
                if landing is not None:
                    value = value + decode(landed[it, h, landing, pl.ds(start, 48), :])
                codes[h, k, pl.ds(start, 48), :] = encode(value)
                return 0

            lax.fori_loop(0, size // 48, some, 0)
            x_copy(it, h, k, s).start()

        def relay(h):
            x_copy(it, h, 0).wait_recv()
            code(h, 4, 1, 0, 0)
            x_copy(it, h, 1).wait_recv()
            code(h, 5, 3, 1, 0)
            code(h, 4, 1, 0, 1)
            code(h, 5, 3, 1, 1)

        def finish(h, s):
            if s == 0:
                for k in (2, 3):
                    x_copy(it, h, k).wait_recv()
            for k in (4, 5):
                x_copy(it, h, k, s).wait_recv()
            for p, pair in enumerate(((3, 4), (2, 5))):
                for a in range(*piece_of(h, p, s)):
                    rows = slice(48 * (a - PARTS[h][p][0]), 48 * (a - PARTS[h][p][0]) + 48)
                    value = product[0, 48 * a : 48 * a + 48, h * H : h * H + H]
                    for k in pair:
                        value = value + decode(landed[it, h, k, rows, :])
                    put = places(h, s)[a]
                    for z in range(4):
                        flat[h, z, put : put + B, :] = value[B * z : B * z + B, :]
            for z in range(4):
                zcodes[h, z, FLAT_ROWS[s], :] = encode(flat[h, z, FLAT_ROWS[s], :])
            for d in (2, 1, 3):
                z_copy(it, h, s, d).start()

        def multiply_whole(n):
            for side in (zh, other):
                value = jnp.dot(folded[(x + n) % 4, side], supply_of(it, side), preferred_element_type=f32)
                product[n] = value if side is zh else product[n] + value

        multiply(2, *part_rows(0, 0))
        code(0, 0, 2)
        multiply(2, *part_rows(0, 1))
        code(0, 1, 2)
        send_halo_rows(it)
        multiply(1)
        code(0, 2, 1)
        code(1, 1, 2)
        multiply_whole(3)
        code(0, 3, 3)
        code(1, 0, 2)
        relay(0)
        code(1, 2, 1)
        code(1, 3, 3)
        multiply_whole(0)
        relay(1)
        finish(0, 0)
        finish(0, 1)
        finish(1, 0)
        finish(1, 1)
        for d in range(4):
            halo_copy(it, d).wait_recv()
        for f, field in enumerate((tech, temp)):
            low = jnp.where(row == 0, 0.0, halo_in[it, 0, f, 0:B, :])
            high = jnp.where(row == 15, 0.0, halo_in[it, 1, f, 0:B, :])
            for a in range(A):
                padded[f, a, 1 : 1 + B, :] = field[a]
                padded[f, a, 0:1, :] = jnp.where(col == 0, 0.0, halo_in[it, 2, f, a : a + 1, :])
                padded[f, a, B + 1 : B + 2, :] = jnp.where(col == 15, 0.0, halo_in[it, 3, f, a : a + 1, :])
            for a in range(A):
                centre = field[a]
                below_ = low if a == 0 else padded[f, a - 1, 1 : 1 + B, :]
                above_ = high if a == A - 1 else padded[f, a + 1, 1 : 1 + B, :]
                lap = above_ + below_ + padded[f, a, 2 : 2 + B, :] + padded[f, a, 0:B, :] - 4.0 * centre
                tech_new[f, a] = centre + 0.2 * lap
        for a in range(A):
            tech_new[0, a] = tech_new[0, a] - 0.05 * temp[a] * temp[a]

        for d in range(4):
            halo_copy(it, d).wait_send()
        for h in (0, 1):
            for copy in gather_copies(it, h):
                copy().wait_send()
            for copy in x_copies(it, h):
                copy.wait_send()
        for h in (0, 1):
            for s in (0, 1):
                for d in (1, 3, 2):
                    z_copy(it, h, s, d).wait_recv()
            lanes = slice(h * H, h * H + H)
            total = flat[h, zl]
            for d in (1, 2, 3):
                total = total + decode(zlanded[it, h, d - 1])
            where = {**places(h, 0), **places(h, 1)}
            for a in range(A):
                target_ = 0.5 * (jnp.log(total[where[a] : where[a] + B, :]) + tech[a, :, lanes])
                wage_a = wage[a, :, lanes] + damping[0] * (target_ - wage[a, :, lanes])
                wage[a, :, lanes] = wage_a
                temp[a, :, lanes] = tech_new[1, a, :, lanes] + 0.5 * share[a, :, lanes] * jnp.tanh(wage_a)
                tech[a, :, lanes] = tech_new[0, a, :, lanes]

            @pl.when(it < ITERS - 1)
            def _():
                send_supply(it + 1, h)

            @pl.when(it == ITERS - 1)
            def _():
                for copy in leave(h):
                    copy.start()

        for h in (0, 1):
            for s in (0, 1):
                for d in (1, 2, 3):
                    z_copy(it, h, s, d).wait_send()

        @pl.when(it < ITERS - 1)
        def _():
            gather(it + 1, multiply_near)

        return 0

    def build(n, halves):
        if n == 0:
            fold(0)
            fold(1)
        elif n == 2:
            fold(2)
            fold(3)
        elif n == 4:
            halves(1, 3)

    pl.semaphore_wait(barrier, len(peers))
    for copy in starts:
        copy.wait()
    send_supply(0, 0)
    send_supply(0, 1)
    gather(0, build)
    lax.fori_loop(0, ITERS, iteration, 0)
    for h in (0, 1):
        for copy in leave(h):
            copy.wait()


def hand_on(*refs):
    sources, results, held, (sem,) = refs[0:3], refs[3:6], refs[6:9], refs[9:]
    into = [pltpu.make_async_copy(sources[n], held[n], sem.at[0, n]) for n in range(3)]
    out = [pltpu.make_async_copy(held[n], results[n], sem.at[1, n]) for n in range(3)]
    for copy in into:
        copy.start()
    for n in range(3):
        into[n].wait()
        out[n].start()
    for copy in out:
        copy.wait()


def local(cost_rough, land_mask, wage_start, tech_start, temp_start, damping):
    field = jax.ShapeDtypeStruct((A, B, S), f32)
    vmem = pl.BlockSpec(memory_space=pltpu.VMEM)
    hbm = pl.BlockSpec(memory_space=pl.ANY)
    dma = pltpu.SemaphoreType.DMA
    fields = pl.pallas_call(
        kernel,
        out_shape=(field, field, field),
        in_specs=[hbm, vmem, hbm, hbm, hbm, pl.BlockSpec(memory_space=pltpu.SMEM)],
        out_specs=(hbm, hbm, hbm),
        scratch_shapes=[
            pltpu.VMEM((A, B, S), f32),
            pltpu.VMEM((A, B, S), f32),
            pltpu.VMEM((A, B, S), f32),
            pltpu.VMEM((A, LON, K), jnp.bfloat16),
            pltpu.VMEM((4, BLOCK, K), jnp.bfloat16),
            pltpu.VMEM((LON, K), f32),
            pltpu.VMEM((2, 16 * PIECE, 16 * PIECE), jnp.bfloat16),
            pltpu.VMEM((4, 2, BLOCK, WIDE), jnp.bfloat16),
            pltpu.VMEM((A, B, S), f32),
            pltpu.VMEM((ITERS, 2, 2, 3, SIDE, H), jnp.bfloat16),
            pltpu.VMEM((2, 3, PIECE, H), f32),
            pltpu.VMEM((4, BLOCK, S), f32),
            pltpu.VMEM((2, 6, 288, H), jnp.int16),
            pltpu.VMEM((ITERS, 2, 6, 288, H), jnp.int16),
            pltpu.VMEM((2, 4, FLAT, H), f32),
            pltpu.VMEM((2, 4, FLAT, H), jnp.int16),
            pltpu.VMEM((ITERS, 2, 3, FLAT, H), jnp.int16),
            pltpu.VMEM((2, A, 16, S), f32),
            pltpu.VMEM((ITERS, 4, 2, 16, S), f32),
            pltpu.VMEM((ITERS, 4, 2, 16, S), f32),
            pltpu.VMEM((2, A, B, S), f32),
            dma((3,)),
            dma((A,)),
            dma((2, 15)), dma((2, 2, 15)),
            dma((2, 8)), dma((2, 2, 8)),
            dma((2, 2, 3)), dma((2, 2, 2, 3)),
            dma((4,)), dma((2, 4)),
        ],
        compiler_params=pltpu.CompilerParams(collective_id=0, has_side_effects=True, vmem_limit_bytes=60 * 1024 * 1024),
    )(cost_rough, land_mask, wage_start, tech_start, temp_start, damping)
    return pl.pallas_call(
        hand_on,
        out_shape=(field, field, field),
        in_specs=[hbm] * 3,
        out_specs=(hbm,) * 3,
        scratch_shapes=[pltpu.VMEM((A, B, S), f32)] * 3 + [dma((2, 3))],
    )(*fields)


def solution(mesh):
    in_specs = (
        P("row", "col"),
        P("row", "col"),
        P("row", "col", None),
        P("row", "col", None),
        P("row", "col", None),
        P(),
    )
    out_specs = (P("row", "col", None), P("row", "col", None), P("row", "col", None))
    return jax.shard_map(local, mesh=mesh, in_specs=in_specs, out_specs=out_specs, check_vma=False)
```

```python
import functools

import jax
import jax.numpy as jnp
from jax import lax
from jax.experimental import pallas as pl
from jax.experimental.pallas import tpu as pltpu
from jax.sharding import PartitionSpec as P

LAT = 176
LON = 192
ITERS = 3
ELL = 44
A = 11
B = 12
S = 256
H = 128
BLOCK = 528
K = 2112
PIECE = 48
SIDE = 8 * PIECE
WIDE = 3 * SIDE
WINDOWS = ((0, 768, 0), (640, 768, 64), (1408, 704, 0))
PARTS = (((0, 6), (6, 11)), ((0, 5), (5, 11)))
FLAT = 144
FLAT_ROWS = (slice(0, 80), slice(80, 144))
MESH = pl.DeviceIdType.MESH
f32 = jnp.float32
STEPS = 1024.0
MIDDLE = 8192.0
LN2 = 0.6931471805599453


def encode(value):
    code = jnp.log(jnp.maximum(value, 1e-30)) * (STEPS / LN2) + MIDDLE
    return jnp.round(jnp.clip(code, -32767.0, 32767.0)).astype(jnp.int32).astype(jnp.int16)


def decode(code):
    return jnp.exp((code.astype(jnp.int32).astype(f32) - MIDDLE) * (LN2 / STEPS))


def kernel(
    rough, mask, wage0, tech0, temp0, damping,
    wage_out, tech_out, temp_out,
    wage, tech, temp, stage, cost, near, pick, folded, share, gathered, piece, product, codes, landed, flat, zcodes, zlanded,
    padded, halo_out, halo_in, tech_new,
    start_sem, stage_sem, ag_send, ag_recv, x_send, x_recv, z_send, z_recv, halo_send, halo_recv,
):
    row, col = lax.axis_index("row"), lax.axis_index("col")
    zh, y, core = row // 8, (row // 2) % 4, row % 2
    x, zl = col // 4, col % 4

    def at_row(zh_, y_, core_):
        return zh_ * 8 + (y_ % 4) * 2 + core_

    def at_col(x_, zl_):
        return (x_ % 4) * 4 + zl_ % 4

    partner = (at_row(zh, y, 1 - core), col)
    across = (at_row(1 - zh, y, core), col)
    y_up, y_down = (at_row(zh, y + 1, core), col), (at_row(zh, y + 3, core), col)
    x_up, x_down = (row, at_col(x + 1, zl)), (row, at_col(x + 3, zl))
    z_peers = [(row, at_col(x, zl + d)) for d in (1, 2, 3)]
    halo_peers = [((row + 1) % 16, col), ((row + 15) % 16, col), (row, (col + 1) % 16), (row, (col + 15) % 16)]
    y_far = (at_row(zh, y + 2, core), col)
    peers = [partner, across, y_up, y_down, y_far, x_up, x_down] + z_peers + halo_peers

    def load_rough(a):
        return pltpu.make_async_copy(rough.at[pl.ds(a * LON, LON), :], stage.at[a], stage_sem.at[a])

    for a in range(A):
        load_rough(a).start()
    barrier = pltpu.get_barrier_semaphore()
    for peer in peers:
        pl.semaphore_signal(barrier, inc=1, device_id=peer, device_id_type=MESH)
    starts = [
        pltpu.make_async_copy(source, field, start_sem.at[n])
        for n, (source, field) in enumerate(((wage0, wage), (tech0, tech), (temp0, temp)))
    ]
    for copy in starts:
        copy.start()
    piece[...] = jnp.zeros_like(piece)
    flat[...] = jnp.zeros_like(flat)
    halo_out[...] = jnp.zeros_like(halo_out)
    diagonal = lax.broadcasted_iota(jnp.int32, (B, B), 0) == lax.broadcasted_iota(jnp.int32, (B, B), 1)
    for a in range(A):
        line = jnp.broadcast_to(mask[a : a + 1, :].astype(f32), (B, B))
        stand = jnp.sum(jnp.where(diagonal, line, 0.0), axis=1, keepdims=True)
        share[a] = jnp.broadcast_to(0.25 + stand, (B, S))

    column = lax.broadcasted_iota(jnp.int32, (1, K), 1)
    local_b = jnp.zeros_like(column)
    for b in range(1, B):
        local_b = local_b + (column >= LAT * b).astype(jnp.int32)
    source_a = column - LAT * local_b
    source_b = col * B + local_b

    def near_rows(i, _):
        start = pl.multiple_of(i * 16, 16)
        rows = i * 16 + lax.broadcasted_iota(jnp.int32, (16, K), 0)
        near[pl.ds(start, 16), :] = jnp.exp(jnp.abs(rows - source_b).astype(f32) * (-1.0 / ELL))
        return 0

    lax.fori_loop(0, LON // 16, near_rows, 0)

    def cost_latitude(a, _):
        load_rough(a).wait()
        lat = jnp.exp(jnp.abs(row * A + a - source_a).astype(f32) * (-1.0 / ELL)) * (1.0 / (ELL * ELL))

        def cost_rows(i, _):
            start = pl.multiple_of(i * 16, 16)
            put = pl.multiple_of(a * 48 + (i % 3) * 16, 16)
            value = stage[a, pl.ds(start, 16), :].astype(f32) * (lat * near[pl.ds(start, 16), :])
            cost[i // 3, pl.ds(put, 16), :] = value.astype(jnp.bfloat16)
            return 0

        return lax.fori_loop(0, LON // 16, cost_rows, 0)

    lax.fori_loop(0, 7, cost_latitude, 0)

    def fold(n):
        for g, (first, count, shift) in enumerate(WINDOWS):
            block = jnp.dot(
                cost[n, :, first : first + count], pick[1 if shift else 0, 0:count, :], preferred_element_type=f32
            ).astype(jnp.bfloat16)
            folded[n, 0, :, g * SIDE : g * SIDE + SIDE] = block[:, 0:SIDE]
            folded[n, 1, :, g * SIDE : g * SIDE + SIDE] = block[:, SIDE : 2 * SIDE]

    def slot(it, h, zh_, y_, core_):
        start = pl.multiple_of(((y_ % 4) * 2 + core_) * PIECE, 16)
        return gathered.at[it, zh_, h, :, pl.ds(start, PIECE), :]

    def ag(it, h, k, ref, peer):
        return pltpu.make_async_remote_copy(
            src_ref=ref, dst_ref=ref, send_sem=ag_send.at[h, k], recv_sem=ag_recv.at[it % 2, h, k],
            device_id=peer, device_id_type=MESH,
        )

    other = 1 - zh

    def gather_copies(it, h):
        own, theirs = slot(it, h, zh, y, core), slot(it, h, other, y, core)
        table = [
            (0, own, across), (1, own, y_up), (2, own, y_down), (3, own, y_far), (4, own, partner),
            (5, theirs, y_up), (6, theirs, y_down), (7, theirs, y_far), (8, theirs, partner),
            (9, slot(it, h, zh, y + 3, core), partner), (10, slot(it, h, zh, y + 1, core), partner),
            (11, slot(it, h, zh, y + 2, core), partner),
            (12, slot(it, h, other, y + 3, core), partner), (13, slot(it, h, other, y + 1, core), partner),
            (14, slot(it, h, other, y + 2, core), partner),
        ]
        return [functools.partial(ag, it, h, *entry) for entry in table]

    def halo_copy(it, d):
        return pltpu.make_async_remote_copy(
            src_ref=halo_out.at[it, d], dst_ref=halo_in.at[it, d],
            send_sem=halo_send.at[d], recv_sem=halo_recv.at[it % 2, d],
            device_id=halo_peers[d], device_id_type=MESH,
        )

    def send_supply(it, h):
        for a in range(A):
            lanes = slice(h * H, h * H + H)
            value = jnp.exp(tech[a, :, lanes] - wage[a, :, lanes]) * share[a, :, lanes]
            for g in range(3):
                piece[h, g, 4 * a : 4 * a + 4, :] = value[4 * g : 4 * g + 4, :]
        start = pl.multiple_of((y * 2 + core) * PIECE, 16)
        gathered[it, zh, h, :, pl.ds(start, PIECE), :] = piece[h].astype(jnp.bfloat16)
        for copy in gather_copies(it, h)[0:5]:
            copy().start()

    def send_halo_rows(it):
        for f, field in enumerate((tech, temp)):
            halo_out[it, 0, f, 0:B, :] = field[A - 1]
            halo_out[it, 1, f, 0:B, :] = field[0]
        for d in (0, 1):
            halo_copy(it, d).start()

    def send_halo_columns(it):
        for f, field in enumerate((tech, temp)):
            for a in range(A):
                halo_out[it, 2, f, a : a + 1, :] = field[a, B - 1 : B, :]
                halo_out[it, 3, f, a : a + 1, :] = field[a, 0:1, :]
        for d in (2, 3):
            halo_copy(it, d).start()

    def supply_of(it, side):
        return jnp.concatenate([gathered[it, side, h].reshape(WIDE, H) for h in (0, 1)], axis=1)

    def gather(it, meanwhile):
        copies = [gather_copies(it, h) for h in (0, 1)]

        def arrived(h, k, zh_, dy, core_, peer):
            ag(it, h, k, slot(it, h, zh_, y + dy, core_), peer).wait_recv()

        def forward(h, *ks):
            for k in ks:
                copies[h][k]().start()

        def beside(h, side, first, then):
            arrived(h, first, side, 3, core, y_down)
            forward(h, then)
            arrived(h, first + 1, side, 1, core, y_up)
            forward(h, then + 1)

        def near_half(n, _):
            product[n] = jnp.dot(folded[(x + n) % 4, zh], supply_of(it, zh), preferred_element_type=f32)
            return 0

        def halves(first, last):
            lax.fori_loop(first, last, near_half, 0)

        for h in (0, 1):
            meanwhile(h, halves)
            beside(h, zh, 1, 9)
            arrived(h, 0, other, 0, core, across)
            forward(h, 5, 6, 7, 8)
            arrived(h, 3, zh, 2, core, y_far)
            forward(h, 11)
        send_halo_columns(it)
        meanwhile(2, halves)
        for h in (0, 1):
            for k, dy in ((4, 0), (9, 3), (10, 1), (11, 2)):
                arrived(h, k, zh, dy, 1 - core, partner)
        meanwhile(3, halves)
        beside(0, other, 5, 12)
        arrived(0, 7, other, 2, core, y_far)
        forward(0, 14)
        beside(1, other, 5, 12)
        arrived(1, 7, other, 2, core, y_far)
        forward(1, 14)
        meanwhile(4, halves)
        for h in (0, 1):
            for k, dy in ((8, 0), (12, 3), (13, 1), (14, 2)):
                arrived(h, k, other, dy, 1 - core, partner)

    def part_rows(h, p):
        first, last = PARTS[h][p]
        return 48 * first, 48 * (last - first)

    def piece_of(h, p, s):
        first, last = PARTS[h][p]
        middle = first + (last - first + 1) // 2
        return ((first, middle), (middle, last))[s]

    def places(h, s):
        latitudes = [a for p in (0, 1) for a in range(*piece_of(h, p, s))]
        return {a: FLAT_ROWS[s].start + B * n for n, a in enumerate(latitudes)}

    def x_rows(h, k, s):
        p = (0, 1, 1, 0, 0, 1)[k]
        first, last = PARTS[h][p] if s is None else piece_of(h, p, s)
        return 48 * (first - PARTS[h][p][0]), 48 * (last - first)

    def x_copy(it, h, k, s=None):
        first, size = x_rows(h, k, s)
        sem = k if s is None else 2 * k - 4 + s
        return pltpu.make_async_remote_copy(
            src_ref=codes.at[h, k, pl.ds(first, size), :], dst_ref=landed.at[it, h, k, pl.ds(first, size), :],
            send_sem=x_send.at[h, sem], recv_sem=x_recv.at[it % 2, h, sem],
            device_id=x_up if k % 2 == 0 else x_down, device_id_type=MESH,
        )

    def x_copies(it, h):
        return [x_copy(it, h, k) for k in range(4)] + [x_copy(it, h, k, s) for k in (4, 5) for s in (0, 1)]

    def z_copy(it, h, s, d):
        rows = pl.ds(FLAT_ROWS[s].start, FLAT_ROWS[s].stop - FLAT_ROWS[s].start)
        return pltpu.make_async_remote_copy(
            src_ref=zcodes.at[h, (zl + d) % 4, rows, :], dst_ref=zlanded.at[it, h, d - 1, rows, :],
            send_sem=z_send.at[h, s, d - 1], recv_sem=z_recv.at[it % 2, h, s, d - 1],
            device_id=z_peers[d - 1], device_id_type=MESH,
        )

    def multiply_near(n, halves):
        if n == 3:
            halves(1, 3)

    def leave(h):
        lanes = pl.ds(h * H, H)
        return [
            pltpu.make_async_copy(field.at[:, :, lanes], result.at[:, :, lanes], stage_sem.at[3 * h + n])
            for n, (field, result) in enumerate(((wage, wage_out), (tech, tech_out), (temp, temp_out)))
        ]

    def iteration(it, _):
        def multiply(n, first=0, size=BLOCK):
            rows = slice(first, first + size)
            product[n, rows] = product[n, rows] + jnp.dot(
                folded[(x + n) % 4, other, rows], supply_of(it, other), preferred_element_type=f32
            )

        def code(h, k, n, landing=None, s=None):
            base = 48 * PARTS[h][(0, 1, 1, 0, 0, 1)[k]][0]
            first, size = x_rows(h, k, s)

            def some(i, _):
                start = pl.multiple_of(first + i * 48, 16)
                value = product[n, pl.ds(base + start, 48), h * H : h * H + H]
                if landing is not None:
                    value = value + decode(landed[it, h, landing, pl.ds(start, 48), :])
                codes[h, k, pl.ds(start, 48), :] = encode(value)
                return 0

            lax.fori_loop(0, size // 48, some, 0)
            x_copy(it, h, k, s).start()

        def relay(h):
            x_copy(it, h, 0).wait_recv()
            code(h, 4, 1, 0, 0)
            x_copy(it, h, 1).wait_recv()
            code(h, 5, 3, 1, 0)
            code(h, 4, 1, 0, 1)
            code(h, 5, 3, 1, 1)

        def finish(h, s):
            if s == 0:
                for k in (2, 3):
                    x_copy(it, h, k).wait_recv()
            for k in (4, 5):
                x_copy(it, h, k, s).wait_recv()
            for p, pair in enumerate(((3, 4), (2, 5))):
                for a in range(*piece_of(h, p, s)):
                    rows = slice(48 * (a - PARTS[h][p][0]), 48 * (a - PARTS[h][p][0]) + 48)
                    value = product[0, 48 * a : 48 * a + 48, h * H : h * H + H]
                    for k in pair:
                        value = value + decode(landed[it, h, k, rows, :])
                    put = places(h, s)[a]
                    for z in range(4):
                        flat[h, z, put : put + B, :] = value[B * z : B * z + B, :]
            for z in range(4):
                zcodes[h, z, FLAT_ROWS[s], :] = encode(flat[h, z, FLAT_ROWS[s], :])
            for d in (2, 1, 3):
                z_copy(it, h, s, d).start()

        def multiply_whole(n):
            for side in (zh, other):
                value = jnp.dot(folded[(x + n) % 4, side], supply_of(it, side), preferred_element_type=f32)
                product[n] = value if side is zh else product[n] + value

        multiply(2, *part_rows(0, 0))
        code(0, 0, 2)
        multiply(2, *part_rows(0, 1))
        code(0, 1, 2)
        send_halo_rows(it)
        multiply(1)
        code(0, 2, 1)
        code(1, 1, 2)
        multiply_whole(3)
        code(0, 3, 3)
        code(1, 0, 2)
        relay(0)
        code(1, 2, 1)
        code(1, 3, 3)
        multiply_whole(0)
        relay(1)
        finish(0, 0)
        finish(0, 1)
        finish(1, 0)
        finish(1, 1)
        for d in range(4):
            halo_copy(it, d).wait_recv()
        for f, field in enumerate((tech, temp)):
            low = jnp.where(row == 0, 0.0, halo_in[it, 0, f, 0:B, :])
            high = jnp.where(row == 15, 0.0, halo_in[it, 1, f, 0:B, :])
            for a in range(A):
                padded[f, a, 1 : 1 + B, :] = field[a]
                padded[f, a, 0:1, :] = jnp.where(col == 0, 0.0, halo_in[it, 2, f, a : a + 1, :])
                padded[f, a, B + 1 : B + 2, :] = jnp.where(col == 15, 0.0, halo_in[it, 3, f, a : a + 1, :])
            for a in range(A):
                centre = field[a]
                below_ = low if a == 0 else padded[f, a - 1, 1 : 1 + B, :]
                above_ = high if a == A - 1 else padded[f, a + 1, 1 : 1 + B, :]
                lap = above_ + below_ + padded[f, a, 2 : 2 + B, :] + padded[f, a, 0:B, :] - 4.0 * centre
                tech_new[f, a] = centre + 0.2 * lap
        for a in range(A):
            tech_new[0, a] = tech_new[0, a] - 0.05 * temp[a] * temp[a]

        for d in range(4):
            halo_copy(it, d).wait_send()
        for h in (0, 1):
            for copy in gather_copies(it, h):
                copy().wait_send()
            for copy in x_copies(it, h):
                copy.wait_send()
        for h in (0, 1):
            for s in (0, 1):
                for d in (1, 3, 2):
                    z_copy(it, h, s, d).wait_recv()
            lanes = slice(h * H, h * H + H)
            total = flat[h, zl]
            for d in (1, 2, 3):
                total = total + decode(zlanded[it, h, d - 1])
            where = {**places(h, 0), **places(h, 1)}
            for a in range(A):
                target_ = 0.5 * (jnp.log(total[where[a] : where[a] + B, :]) + tech[a, :, lanes])
                wage_a = wage[a, :, lanes] + damping[0] * (target_ - wage[a, :, lanes])
                wage[a, :, lanes] = wage_a
                temp[a, :, lanes] = tech_new[1, a, :, lanes] + 0.5 * share[a, :, lanes] * jnp.tanh(wage_a)
                tech[a, :, lanes] = tech_new[0, a, :, lanes]

            @pl.when(it < ITERS - 1)
            def _():
                send_supply(it + 1, h)

            @pl.when(it == ITERS - 1)
            def _():
                for copy in leave(h):
                    copy.start()

        for h in (0, 1):
            for s in (0, 1):
                for d in (1, 2, 3):
                    z_copy(it, h, s, d).wait_send()

        @pl.when(it < ITERS - 1)
        def _():
            gather(it + 1, multiply_near)

        return 0

    def build(n, halves):
        if n == 0:
            fold(0)
            fold(1)
        elif n == 2:
            fold(2)
            fold(3)
        elif n == 4:
            halves(1, 3)

    pl.semaphore_wait(barrier, len(peers))
    for copy in starts:
        copy.wait()
    send_supply(0, 0)
    send_supply(0, 1)

    spot = lax.broadcasted_iota(jnp.int32, (1, 16 * PIECE), 1)
    device = jnp.zeros_like(spot)
    for r in range(1, 16):
        device = device + (spot >= PIECE * r).astype(jnp.int32)
    rest = spot - PIECE * device
    target = (rest & 3) * LAT + A * device + (rest >> 2)
    target = jnp.where(rest < 4 * A, target, -4096)

    def pick_rows(i, _):
        start = pl.multiple_of(i * 16, 16)
        rows = i * 16 + lax.broadcasted_iota(jnp.int32, (16, 16 * PIECE), 0)
        for n, shift in enumerate((0, 64)):
            pick[n, pl.ds(start, 16), :] = jnp.where(rows == target + shift, 1.0, 0.0).astype(jnp.bfloat16)
        return 0

    lax.fori_loop(0, PIECE, pick_rows, 0)

    lax.fori_loop(7, A, cost_latitude, 0)
    gather(0, build)
    lax.fori_loop(0, ITERS, iteration, 0)
    for h in (0, 1):
        for copy in leave(h):
            copy.wait()


def hand_on(*refs):
    sources, results, held, (sem,) = refs[0:3], refs[3:6], refs[6:9], refs[9:]
    into = [pltpu.make_async_copy(sources[n], held[n], sem.at[0, n]) for n in range(3)]
    out = [pltpu.make_async_copy(held[n], results[n], sem.at[1, n]) for n in range(3)]
    for copy in into:
        copy.start()
    for n in range(3):
        into[n].wait()
        out[n].start()
    for copy in out:
        copy.wait()


def local(cost_rough, land_mask, wage_start, tech_start, temp_start, damping):
    field = jax.ShapeDtypeStruct((A, B, S), f32)
    vmem = pl.BlockSpec(memory_space=pltpu.VMEM)
    hbm = pl.BlockSpec(memory_space=pl.ANY)
    dma = pltpu.SemaphoreType.DMA
    fields = pl.pallas_call(
        kernel,
        out_shape=(field, field, field),
        in_specs=[hbm, vmem, hbm, hbm, hbm, pl.BlockSpec(memory_space=pltpu.SMEM)],
        out_specs=(hbm, hbm, hbm),
        scratch_shapes=[
            pltpu.VMEM((A, B, S), f32),
            pltpu.VMEM((A, B, S), f32),
            pltpu.VMEM((A, B, S), f32),
            pltpu.VMEM((A, LON, K), jnp.bfloat16),
            pltpu.VMEM((4, BLOCK, K), jnp.bfloat16),
            pltpu.VMEM((LON, K), f32),
            pltpu.VMEM((2, 16 * PIECE, 16 * PIECE), jnp.bfloat16),
            pltpu.VMEM((4, 2, BLOCK, WIDE), jnp.bfloat16),
            pltpu.VMEM((A, B, S), f32),
            pltpu.VMEM((ITERS, 2, 2, 3, SIDE, H), jnp.bfloat16),
            pltpu.VMEM((2, 3, PIECE, H), f32),
            pltpu.VMEM((4, BLOCK, S), f32),
            pltpu.VMEM((2, 6, 288, H), jnp.int16),
            pltpu.VMEM((ITERS, 2, 6, 288, H), jnp.int16),
            pltpu.VMEM((2, 4, FLAT, H), f32),
            pltpu.VMEM((2, 4, FLAT, H), jnp.int16),
            pltpu.VMEM((ITERS, 2, 3, FLAT, H), jnp.int16),
            pltpu.VMEM((2, A, 16, S), f32),
            pltpu.VMEM((ITERS, 4, 2, 16, S), f32),
            pltpu.VMEM((ITERS, 4, 2, 16, S), f32),
            pltpu.VMEM((2, A, B, S), f32),
            dma((3,)),
            dma((A,)),
            dma((2, 15)), dma((2, 2, 15)),
            dma((2, 8)), dma((2, 2, 8)),
            dma((2, 2, 3)), dma((2, 2, 2, 3)),
            dma((4,)), dma((2, 4)),
        ],
        compiler_params=pltpu.CompilerParams(collective_id=0, has_side_effects=True, vmem_limit_bytes=60 * 1024 * 1024),
    )(cost_rough, land_mask, wage_start, tech_start, temp_start, damping)
    return pl.pallas_call(
        hand_on,
        out_shape=(field, field, field),
        in_specs=[hbm] * 3,
        out_specs=(hbm,) * 3,
        scratch_shapes=[pltpu.VMEM((A, B, S), f32)] * 3 + [dma((2, 3))],
    )(*fields)


def solution(mesh):
    in_specs = (
        P("row", "col"),
        P("row", "col"),
        P("row", "col", None),
        P("row", "col", None),
        P("row", "col", None),
        P(),
    )
    out_specs = (P("row", "col", None), P("row", "col", None), P("row", "col", None))
    return jax.shard_map(local, mesh=mesh, in_specs=in_specs, out_specs=out_specs, check_vma=False)
```
